128 devices in a mesh: wide: 16 (over x, y_lo, core), narrow: 8 (over y_hi, z).
Axes of the slice: x: 4, y: 4 (y_hi: 2, y_lo: 2; y = y_hi * 2 + y_lo), z: 4, core: 2. Of those that a mesh axis runs over, the one named last changes fastest.
Arguments:
- fit_rows: bfloat16 [3072, 49152], P('narrow', 'wide'), may hold values from -0.0546875 to 0.0546875
- trials: bfloat16 [32, 49152], P(None, 'wide'), may hold values from -6 to 6
- occ_energy: float32 [64], replicated, may hold values from -1.2 to -0.3
- vir_energy: float32 [768], replicated, may hold values from 0.1 to 2
Outputs:
- sigma: float32 [32, 49152], P(None, 'wide')
The draws below stay inside these ranges and needn't reach their ends.
All inputs are finite; a program needn't handle non-finite values.
Results may differ from the reference program's by a relative error of at most 0.004.
Values may be sent and summed in bfloat16 or wider, within the bound.
No kernel may reach another device: no remote copies, remote signals or barrier semaphores. Data moves between devices by JAX's collectives and lax.ppermute only.
A program may use at most 64 MiB of HBM per device.

```python
import math
import jax
import jax.numpy as jnp
from jax import lax

NOCC = 64
NVIR = 768
NAUX = 3072
NVEC = 32
NPAIR = 49152


def block_scale(stream_key, extent, pieces, low, top_value):
    level = 1.0
    for position, parts in pieces:
        draws = jax.random.uniform(jax.random.fold_in(jax.random.fold_in(stream_key, 6), position), (parts,), jnp.float32, low / len(pieces), top_value / len(pieces))
        level = level * jnp.repeat(jnp.exp(draws), extent[position] // parts).reshape((-1,) + (1,) * (len(extent) - 1 - position))
    return level


def normal_values(rng, shape, spread, most, shards=(), kind=jnp.bfloat16):
    result = jax.random.normal(rng, shape, jnp.float32) * spread
    if len(shards) > 0:
        result = block_scale(rng, shape, shards, -0.22, 0.18) * result
    return jnp.clip(result, min=-most, max=most).astype(kind)


def setup_inputs(seed: int = 0) -> dict:
    key_list = jax.random.split(jax.random.key(seed), 5)
    fit_rows = normal_values(key_list[0], (NAUX, NPAIR), (4 * NAUX) ** -0.5, 0.0546875, ((0, 8), (1, 16)))
    trials = normal_values(key_list[1], (NVEC, NPAIR), 1.0, 6.0, ((1, 16),))
    occ_energy = jnp.clip(jax.random.uniform(key_list[2], (NOCC,), jnp.float32, -1.2, -0.3), -1.2, -0.3)
    vir_energy = jnp.clip(jax.random.uniform(key_list[3], (NVIR,), jnp.float32, 0.1, 2.0), 0.1, 2.0)
    return {"fit_rows": fit_rows, "trials": trials, "occ_energy": occ_energy, "vir_energy": vir_energy}


def reference(fit_rows, trials, occ_energy, vir_energy):
    fitvec = lax.dot_general(fit_rows, trials, (((1,), (1,)), ((), ())), preferred_element_type=jnp.float32)
    fitvec_b = fitvec.astype(jnp.bfloat16)
    coulomb = 2.0 * lax.dot_general(fitvec_b, fit_rows, (((0,), (0,)), ((), ())), preferred_element_type=jnp.float32)
    block = math.gcd(NAUX, 64)
    blocks = fit_rows.reshape(NAUX // block, block, NOCC, NVIR)
    vectors = trials.astype(jnp.float32).reshape(NVEC, NOCC, NVIR)

    def step(carry, rows):
        rows32 = rows.astype(jnp.float32)
        inter = jnp.einsum("pib,njb->pnij", rows32, vectors).astype(jnp.bfloat16)
        term = jnp.einsum("pnij,pja->nia", inter.astype(jnp.float32), rows32)
        return carry + term, None

    exchange, _ = lax.scan(step, jnp.zeros((NVEC, NOCC, NVIR), jnp.float32), blocks)
    delta = (vir_energy[None, :] - occ_energy[:, None]).reshape(NOCC * NVIR)
    return delta[None, :] * trials.astype(jnp.float32) + coulomb - exchange.reshape(NVEC, NOCC * NVIR)
```

```python
import jax
import jax.numpy as jnp
from jax import lax
from jax.experimental import pallas as pl
from jax.experimental.pallas import tpu as pltpu
from jax.sharding import Mesh, PartitionSpec as P

NOCC = 64
NVIR = 768
NVEC = 32
NCHIP = 8
OCC_DEV = 4
HALF = 16
CHUNKS = 3
ROWS = NOCC * HALF

F32 = jnp.float32
BF16 = jnp.bfloat16


def swap_blocks(tile):
    v = [tile[j * 16 : (j + 1) * 16] for j in range(8)]
    lane = lax.broadcasted_iota(jnp.int32, (16, 128), 1)
    for s in (4, 2, 1):
        bit = (lane & (16 * s)) != 0
        new = list(v)
        for j in range(8):
            if j & s:
                continue
            lo, hi = v[j], v[j + s]
            new[j] = jnp.where(bit, pltpu.roll(hi, 16 * s, 1), lo)
            new[j + s] = jnp.where(bit, hi, pltpu.roll(lo, 128 - 16 * s, 1))
        v = new
    return v


def chunk_kernel(first, last, *refs):
    if first:
        core, xg, b_own, b_other, out, x2, b2, d, c_buf, fit, sems = refs
        acc = out
    elif last:
        core, xg, b_own, b_other, acc, out, x2, b2, d, c_buf, fit, sems = refs
    else:
        core, xg, b_own, b_other, acc, out, x2, b2, d, c_buf, fit, sems = refs
    c = core[0]
    copies = []
    for rel in range(2):
        src_b = b_own if rel == 0 else b_other
        for chip in range(NCHIP):
            for q in range(OCC_DEV):
                row = ((rel * NCHIP + chip) * OCC_DEV + q) * 16
                copies.append(pltpu.make_async_copy(src_b.at[chip, :, pl.ds(q * NVIR, NVIR)], b2.at[pl.ds(row, 16), :], sems.at[0]))
                w = chip * 2 + (c ^ rel)
                copies.append(pltpu.make_async_copy(xg.at[w, :, pl.ds(q * NVIR, NVIR)], x2.at[pl.ds(row, 16), :], sems.at[0]))
    for cp in copies:
        cp.start()
    for cp in copies:
        cp.wait()
    row_i = lax.broadcasted_iota(jnp.int32, (128, 128), 0) // 16
    lane_i = lax.broadcasted_iota(jnp.int32, (128, 128), 1) // 16
    diag = row_i == lane_i
    fit[...] = jnp.zeros_like(fit)

    @pl.loop(0, 4)
    def _(ig2):
        rhs = b2[pl.ds(pl.multiple_of(ig2 * 256, 256), 256), :]
        c_buf[...] = lax.dot_general(x2[...], rhs, (((1,), (1,)), ((), ())), preferred_element_type=F32)
        for half in range(2):
            ig = ig2 * 2 + half
            own = c_buf[pl.ds(pl.multiple_of(ig * 128, 128), 128), half * 128 : (half + 1) * 128]
            fit[...] += jnp.where(diag, own, 0.0)
            for jg in range(8):
                tile = c_buf[jg * 128 : (jg + 1) * 128, half * 128 : (half + 1) * 128]
                t = swap_blocks(tile)
                d[pl.ds(pl.multiple_of(ig * 128, 128), 128), jg * 128 : (jg + 1) * 128] = jnp.concatenate(t, 0).astype(BF16)

    total = fit[0:16, :]
    for j in range(1, 8):
        total = total + fit[j * 16 : (j + 1) * 16, :]
    for s in (64, 32, 16):
        total = total + pltpu.roll(total, s, 1)
    fit_b = 2.0 * total.astype(BF16).astype(F32)
    sub = jnp.where(diag, jnp.concatenate([fit_b] * 8, 0), 0.0)
    for g in range(8):
        s = slice(g * 128, (g + 1) * 128)
        d[s, s] = (d[s, s].astype(F32) - sub).astype(BF16)

    for rb in range(4):
        rows = slice(rb * 256, (rb + 1) * 256)
        term = jnp.dot(d[rows, :], b2[...], preferred_element_type=F32)
        if not first:
            term = term + acc[rows, :]
        if not last:
            out[rows, :] = term
        else:
            for k in range(16):
                i = rb * 16 + k
                rel, chip, q = i // 32, (i // 4) % 8, i % 4
                w = chip * 2 + (c ^ rel)
                out[w, :, q * NVIR : (q + 1) * NVIR] = term[k * 16 : (k + 1) * 16, :].astype(BF16)


def chunk(core, xg, b_own, b_other, acc, last):
    first = acc is None
    hbm = pl.BlockSpec(memory_space=pl.ANY)
    vmem = pl.BlockSpec(memory_space=pltpu.VMEM)
    args = [core, xg, b_own, b_other] + ([] if first else [acc])
    specs = [pl.BlockSpec(memory_space=pltpu.SMEM), hbm, hbm, hbm] + ([] if first else [vmem])
    out = jax.ShapeDtypeStruct((16, HALF, OCC_DEV * NVIR), BF16) if last else jax.ShapeDtypeStruct((ROWS, NVIR), F32)
    flops = 2 * 2 * ROWS * ROWS * NVIR
    return pl.pallas_call(
        lambda *refs: chunk_kernel(first, last, *refs),
        out_shape=out,
        in_specs=specs,
        out_specs=vmem,
        scratch_shapes=[
            pltpu.VMEM((ROWS, NVIR), BF16),
            pltpu.VMEM((ROWS, NVIR), BF16),
            pltpu.VMEM((ROWS, ROWS), BF16),
            pltpu.VMEM((ROWS, 256), F32),
            pltpu.VMEM((128, 128), F32),
            pltpu.SemaphoreType.DMA((1,)),
        ],
        cost_estimate=pl.CostEstimate(flops=flops, bytes_accessed=4 * ROWS * NVIR * 2, transcendentals=0),
        compiler_params=pltpu.CompilerParams(vmem_limit_bytes=40 << 20),
        name="terms_last" if last else "terms_first" if first else "terms_mid",
    )(*args)


CHIPS = ("x", "yl")
WIDE = ("x", "yl", "c")
NARROW = ("yh", "z")


def local(fit_rows, trials, occ_energy, vir_energy):
    core = lax.axis_index("c").astype(jnp.int32).reshape(1)
    blocks = fit_rows.reshape(CHUNKS, NCHIP, HALF, OCC_DEV * NVIR)
    own = [lax.all_to_all(blocks[t], CHIPS, 0, 0, tiled=True) for t in range(CHUNKS)]
    other = [lax.ppermute(own[t], "c", [(0, 1), (1, 0)]) for t in range(CHUNKS)]
    halves = trials.reshape(1, 2, HALF, OCC_DEV * NVIR)
    send = jnp.broadcast_to(halves, (NCHIP, 2, HALF, OCC_DEV * NVIR)).reshape(16, HALF, OCC_DEV * NVIR)
    xg = lax.all_to_all(send, WIDE, 0, 0, tiled=True)
    acc = None
    for t in range(CHUNKS):
        acc = chunk(core, xg, own[t], other[t], acc, t == CHUNKS - 1)
    parts = lax.all_to_all(acc, WIDE, 0, 0, tiled=True)
    part = jnp.sum(parts.reshape(NCHIP, 2 * HALF, OCC_DEV * NVIR).astype(F32), 0).astype(BF16)
    every = lax.all_to_all(jnp.broadcast_to(part[None], (8, NVEC, OCC_DEV * NVIR)), NARROW, 0, 0, tiled=True)
    total = jnp.sum(every.astype(F32), 0)
    w = lax.axis_index(WIDE)
    occ = lax.dynamic_slice_in_dim(occ_energy, w * OCC_DEV, OCC_DEV)
    delta = (vir_energy[None, :] - occ[:, None]).reshape(OCC_DEV * NVIR)
    return delta[None, :] * trials.astype(F32) - total


def solution(mesh):
    fine = Mesh(mesh.devices.reshape(4, 2, 2, 2, 4), ("x", "yl", "c", "yh", "z"))
    in_specs = (P(NARROW, WIDE), P(None, WIDE), P(), P())
    return jax.shard_map(local, mesh=fine, in_specs=in_specs, out_specs=P(None, WIDE), check_vma=False)
```

```python
import jax
import jax.numpy as jnp
from jax import lax
from jax.experimental import pallas as pl
from jax.experimental.pallas import tpu as pltpu
from jax.sharding import Mesh, PartitionSpec as P

NOCC = 64
NVIR = 768
NVEC = 32
NCHIP = 8
OCC_DEV = 4
HALF = 16
CHUNKS = 3
ROWS = NOCC * HALF
PIECE = NVIR // 2

F32 = jnp.float32
BF16 = jnp.bfloat16


def swap_blocks(tile):
    v = [tile[j * 16 : (j + 1) * 16] for j in range(8)]
    lane = lax.broadcasted_iota(jnp.int32, (16, 128), 1)
    for s in (4, 2, 1):
        bit = (lane & (16 * s)) != 0
        new = list(v)
        for j in range(8):
            if j & s:
                continue
            lo, hi = v[j], v[j + s]
            new[j] = jnp.where(bit, pltpu.roll(hi, 16 * s, 1), lo)
            new[j + s] = jnp.where(bit, hi, pltpu.roll(lo, 128 - 16 * s, 1))
        v = new
    return v


def chunk_kernel(first, last, *refs):
    where, xq, b_own, b_other = refs[0], refs[1:5], refs[5], refs[6]
    acc = None if first else refs[7]
    out, x2, b2, d, c_buf, fit, sems = refs[-7:]
    c, z = where[0], where[1]
    copies = []
    for rel in range(2):
        src_b = b_own if rel == 0 else b_other
        for chip in range(NCHIP):
            w = chip * 2 + (c ^ rel)
            for q in range(OCC_DEV):
                base = (rel * NCHIP + chip) * OCC_DEV
                row = (base + q) * 16
                copies.append(pltpu.make_async_copy(src_b.at[chip, :, pl.ds(q * NVIR, NVIR)], b2.at[pl.ds(row, 16), :], sems.at[0]))
                row = pl.multiple_of((base + ((z - q) & 3)) * 16, 16)
                copies.append(pltpu.make_async_copy(xq[q].at[w], x2.at[pl.ds(row, 16), :], sems.at[0]))
    for cp in copies:
        cp.start()
    for cp in copies:
        cp.wait()
    row_i = lax.broadcasted_iota(jnp.int32, (128, 128), 0) // 16
    lane_i = lax.broadcasted_iota(jnp.int32, (128, 128), 1) // 16
    diag = row_i == lane_i
    fit[...] = jnp.zeros_like(fit)

    @pl.loop(0, 4)
    def _(ig2):
        rhs = b2[pl.ds(pl.multiple_of(ig2 * 256, 256), 256), :]
        c_buf[...] = lax.dot_general(x2[...], rhs, (((1,), (1,)), ((), ())), preferred_element_type=F32)
        for half in range(2):
            ig = ig2 * 2 + half
            own = c_buf[pl.ds(pl.multiple_of(ig * 128, 128), 128), half * 128 : (half + 1) * 128]
            fit[...] += jnp.where(diag, own, 0.0)
            for jg in range(8):
                tile = c_buf[jg * 128 : (jg + 1) * 128, half * 128 : (half + 1) * 128]
                t = swap_blocks(tile)
                d[pl.ds(pl.multiple_of(ig * 128, 128), 128), jg * 128 : (jg + 1) * 128] = jnp.concatenate(t, 0).astype(BF16)

    total = fit[0:16, :]
    for j in range(1, 8):
        total = total + fit[j * 16 : (j + 1) * 16, :]
    for s in (64, 32, 16):
        total = total + pltpu.roll(total, s, 1)
    fit_b = 2.0 * total.astype(BF16).astype(F32)
    sub = jnp.where(diag, jnp.concatenate([fit_b] * 8, 0), 0.0)
    for g in range(8):
        s = slice(g * 128, (g + 1) * 128)
        d[s, s] = (d[s, s].astype(F32) - sub).astype(BF16)

    for rb in range(4):
        rows = slice(rb * 256, (rb + 1) * 256)
        term = jnp.dot(d[rows, :], b2[...], preferred_element_type=F32)
        if not first:
            term = term + acc[rows, :]
        if not last:
            out[rows, :] = term
        else:
            for k in range(16):
                i = rb * 16 + k
                rel, chip, q = i // 32, (i // 4) % 8, i % 4
                w = chip * 2 + (c ^ rel)
                for h in range(2):
                    out[h * OCC_DEV + q, w] = term[k * 16 : (k + 1) * 16, h * PIECE : (h + 1) * PIECE].astype(BF16)


def chunk(where, xq, b_own, b_other, acc, last):
    first = acc is None
    hbm = pl.BlockSpec(memory_space=pl.ANY)
    vmem = pl.BlockSpec(memory_space=pltpu.VMEM)
    args = [where, *xq, b_own, b_other] + ([] if first else [acc])
    specs = [pl.BlockSpec(memory_space=pltpu.SMEM)] + [hbm] * 6 + ([] if first else [vmem])
    out = jax.ShapeDtypeStruct((8, 16, HALF, PIECE), BF16) if last else jax.ShapeDtypeStruct((ROWS, NVIR), F32)
    flops = 2 * 2 * ROWS * ROWS * NVIR
    return pl.pallas_call(
        lambda *refs: chunk_kernel(first, last, *refs),
        out_shape=out,
        in_specs=specs,
        out_specs=vmem,
        scratch_shapes=[
            pltpu.VMEM((ROWS, NVIR), BF16),
            pltpu.VMEM((ROWS, NVIR), BF16),
            pltpu.VMEM((ROWS, ROWS), BF16),
            pltpu.VMEM((ROWS, 256), F32),
            pltpu.VMEM((128, 128), F32),
            pltpu.SemaphoreType.DMA((1,)),
        ],
        cost_estimate=pl.CostEstimate(flops=flops, bytes_accessed=4 * ROWS * NVIR * 2, transcendentals=0),
        compiler_params=pltpu.CompilerParams(vmem_limit_bytes=24 << 20),
        name="terms_last" if last else "terms_first" if first else "terms_mid",
    )(*args)


CHIPS = ("x", "yl")
WIDE = ("x", "yl", "c")
NARROW = ("yh", "z")


def body(fit_rows, trials, occ_energy, vir_energy):
    core = lax.axis_index("c").astype(jnp.int32)
    z = lax.axis_index("z").astype(jnp.int32)
    where = jnp.stack([core, z])
    mine = lax.dynamic_slice_in_dim(trials, z * NVIR, NVIR, 1).reshape(1, 2, HALF, NVIR)
    send = jnp.broadcast_to(mine, (NCHIP, 2, HALF, NVIR)).reshape(16, HALF, NVIR)
    xq = [lax.all_to_all(send, WIDE, 0, 0, tiled=True)]
    for s in (1, 2, 3):
        xq.append(lax.ppermute(xq[0], "z", [(i, (i + s) % 4) for i in range(4)]))
    blocks = fit_rows.reshape(CHUNKS, NCHIP, HALF, OCC_DEV * NVIR)
    own, other = [], []
    for t in range(CHUNKS):
        own.append(lax.all_to_all(blocks[t], CHIPS, 0, 0, tiled=True))
        other.append(lax.ppermute(own[t], "c", [(0, 1), (1, 0)]))
    acc = None
    for t in range(CHUNKS):
        acc = chunk(where, xq, own[t], other[t], acc, t == CHUNKS - 1)
    parts = lax.all_to_all(acc, NARROW, 0, 0, tiled=True)
    part = jnp.sum(parts.astype(F32), 0).astype(BF16)
    parts = lax.all_to_all(part, WIDE, 0, 0, tiled=True)
    part = jnp.sum(parts.reshape(NCHIP, NVEC, PIECE).astype(F32), 0).astype(BF16)
    every = lax.all_to_all(jnp.broadcast_to(part[None], (8, NVEC, PIECE)), NARROW, 0, 0, tiled=True)
    total = every.reshape(2, OCC_DEV, NVEC, PIECE).transpose(2, 1, 0, 3).reshape(NVEC, OCC_DEV * NVIR)
    w = lax.axis_index(WIDE)
    occ = lax.dynamic_slice_in_dim(occ_energy, w * OCC_DEV, OCC_DEV)
    delta = (vir_energy[None, :] - occ[:, None]).reshape(OCC_DEV * NVIR)
    return delta[None, :] * trials.astype(F32) - total.astype(F32)


def solution(mesh):
    fine = Mesh(mesh.devices.reshape(4, 2, 2, 2, 4), ("x", "yl", "c", "yh", "z"))
    in_specs = (P(NARROW, WIDE), P(None, WIDE), P(), P())
    return jax.shard_map(body, mesh=fine, in_specs=in_specs, out_specs=P(None, WIDE), check_vma=False)
```

```python
import jax
import jax.numpy as jnp
from jax import lax
from jax.experimental import pallas as pl
from jax.experimental.pallas import tpu as pltpu
from jax.sharding import Mesh, PartitionSpec as P

NOCC = 64
NVIR = 768
NVEC = 32
NCHIP = 8
OCC_DEV = 4
PAIRS = OCC_DEV * NVIR
HALF = 16
CHUNKS = 3
ROWS = NOCC * HALF

F32 = jnp.float32
BF16 = jnp.bfloat16

CHIPS = ("x", "yl")
WIDE = ("x", "yl", "c")
NARROW = ("yh", "z")
MOST = ("x", "yl", "c", "z")


def swap_blocks(tile):
    v = [tile[j * 16 : (j + 1) * 16] for j in range(8)]
    lane = lax.broadcasted_iota(jnp.int32, (16, 128), 1)
    for s in (4, 2, 1):
        bit = (lane & (16 * s)) != 0
        new = list(v)
        for j in range(8):
            if j & s:
                continue
            lo, hi = v[j], v[j + s]
            new[j] = jnp.where(bit, pltpu.roll(hi, 16 * s, 1), lo)
            new[j + s] = jnp.where(bit, hi, pltpu.roll(lo, 128 - 16 * s, 1))
        v = new
    return jnp.concatenate(v, 0)


def gather_rows(b2, b_own, b_other):
    for rel, src in enumerate((b_own, b_other)):
        for chip in range(NCHIP):
            for q in range(OCC_DEV):
                row = ((rel * NCHIP + chip) * OCC_DEV + q) * 16
                b2[row : row + 16, :] = src[chip, :, q * NVIR : (q + 1) * NVIR]


def contract_first(x2, b2, d):
    row_i = lax.broadcasted_iota(jnp.int32, (128, 128), 0) // 16
    lane_i = lax.broadcasted_iota(jnp.int32, (128, 128), 1) // 16
    diag = row_i == lane_i
    fit = jnp.zeros((128, 128), F32)
    for g in range(4):
        rhs = b2[g * 256 : (g + 1) * 256, :]
        for rb in range(4):
            lhs = x2[rb * 256 : (rb + 1) * 256, :]
            inter = lax.dot_general(lhs, rhs, (((1,), (1,)), ((), ())), preferred_element_type=F32)
            for a in range(2):
                for h in range(2):
                    ig, jg = g * 2 + h, rb * 2 + a
                    tile = inter[a * 128 : (a + 1) * 128, h * 128 : (h + 1) * 128]
                    if ig == jg:
                        fit = fit + jnp.where(diag, tile, 0.0)
                    d[ig * 128 : (ig + 1) * 128, jg * 128 : (jg + 1) * 128] = swap_blocks(tile).astype(BF16)
    total = fit[0:16, :]
    for j in range(1, 8):
        total = total + fit[j * 16 : (j + 1) * 16, :]
    for s in (64, 32, 16):
        total = total + pltpu.roll(total, s, 1)
    fit_b = 2.0 * total.astype(BF16).astype(F32)
    sub = jnp.where(diag, jnp.concatenate([fit_b] * 8, 0), 0.0)
    for g in range(8):
        s = slice(g * 128, (g + 1) * 128)
        d[s, s] = (d[s, s].astype(F32) - sub).astype(BF16)


def early_kernel(where, x_a, x_b, x_c, x_d, own0, other0, own1, other1, out, x_out, x2, b2, d, acc, sems):
    z = where[1]
    for s, ref in enumerate((x_a, x_b, x_c, x_d)):
        q = (z - s) & 3
        for k in range(16):
            row = pl.multiple_of((k * OCC_DEV + q) * 16, 16)
            x2[pl.ds(row, 16), :] = ref[k // NCHIP, k % NCHIP]
    keep_x = pltpu.make_async_copy(x2, x_out, sems.at[0])
    keep_x.start()
    copies = []
    for t, (own, other) in enumerate(((own0, other0), (own1, other1))):
        gather_rows(b2, own, other)
        contract_first(x2, b2, d)
        for rb in range(4):
            rows = slice(rb * 256, (rb + 1) * 256)
            term = jnp.dot(d[rows, :], b2[...], preferred_element_type=F32)
            if t == 0:
                acc[rows, :] = term
            else:
                acc[rows, :] += term
                copies.append(pltpu.make_async_copy(acc.at[rows], out.at[rows], sems.at[1 + rb]))
                copies[-1].start()
    keep_x.wait()
    for cp in copies:
        cp.wait()


def late_kernel(where, x_in, own, other, acc_in, out, x2, b2, d, acc, sems):
    c = where[0]
    get_x = pltpu.make_async_copy(x_in, x2, sems.at[0])
    get_x.start()
    get_acc = pltpu.make_async_copy(acc_in, acc, sems.at[1])
    get_acc.start()
    gather_rows(b2, own, other)
    get_x.wait()
    contract_first(x2, b2, d)
    get_acc.wait()
    for rb in range(4):
        rows = slice(rb * 256, (rb + 1) * 256)
        term = acc[rows, :] + jnp.dot(d[rows, :], b2[...], preferred_element_type=F32)
        for k in range(16):
            i = rb * 16 + k
            rel, chip, q = i // 32, (i // 4) % 8, i % 4
            w = chip * 2 + (c ^ rel)
            out[w * OCC_DEV + q] = term[k * 16 : (k + 1) * 16, :].astype(BF16)


SMEM = pl.BlockSpec(memory_space=pltpu.SMEM)
VMEM = pl.BlockSpec(memory_space=pltpu.VMEM)
HBM = pl.BlockSpec(memory_space=pltpu.HBM)
SCRATCH = [
    pltpu.VMEM((ROWS, NVIR), BF16),
    pltpu.VMEM((ROWS, NVIR), BF16),
    pltpu.VMEM((ROWS, ROWS), BF16),
    pltpu.VMEM((ROWS, NVIR), F32),
    pltpu.SemaphoreType.DMA((5,)),
]


def cost(count):
    return pl.CostEstimate(flops=count * 4 * ROWS * ROWS * NVIR, bytes_accessed=4 * ROWS * NVIR * 2, transcendentals=0)


def early(where, x, own, other):
    return pl.pallas_call(
        early_kernel,
        out_shape=[jax.ShapeDtypeStruct((ROWS, NVIR), F32), jax.ShapeDtypeStruct((ROWS, NVIR), BF16)],
        in_specs=[SMEM] + [VMEM] * 8,
        out_specs=[HBM, HBM],
        scratch_shapes=SCRATCH,
        cost_estimate=cost(2),
        compiler_params=pltpu.CompilerParams(vmem_limit_bytes=32 << 20),
        name="terms_early",
    )(where, *x, own[0], other[0], own[1], other[1])


def late(where, x2, own, other, acc):
    return pl.pallas_call(
        late_kernel,
        out_shape=jax.ShapeDtypeStruct((16 * OCC_DEV, HALF, NVIR), BF16),
        in_specs=[SMEM, HBM, VMEM, VMEM, HBM],
        out_specs=VMEM,
        scratch_shapes=SCRATCH,
        cost_estimate=cost(1),
        compiler_params=pltpu.CompilerParams(vmem_limit_bytes=32 << 20),
        name="terms_late",
    )(where, x2, own[2], other[2], acc)


def ring(n, s):
    return [(i, (i + s) % n) for i in range(n)]


def body(fit_rows, trials, occ_energy, vir_energy):
    core = lax.axis_index("c").astype(jnp.int32)
    z = lax.axis_index("z").astype(jnp.int32)
    where = jnp.stack([core, z])
    blocks = fit_rows.reshape(CHUNKS, NCHIP, HALF, PAIRS)
    mine = lax.dynamic_slice_in_dim(trials, z * NVIR, NVIR, 1)
    mine = jnp.concatenate([mine[:HALF], mine[HALF:]], 1)
    mine = jnp.broadcast_to(mine[None], (NCHIP, HALF, 2 * NVIR))
    own, other = [], []
    for t in range(CHUNKS):
        send = blocks[t]
        if t == 0:
            send = jnp.concatenate([send, mine], 2)
        own.append(lax.all_to_all(send, CHIPS, 0, 0, tiled=True))
        other.append(lax.ppermute(own[t], "c", ring(2, 1)))
    x_own = lax.dynamic_slice_in_dim(own[0], PAIRS + core * NVIR, NVIR, 2)
    x_send = lax.dynamic_slice_in_dim(own[0], PAIRS + (1 - core) * NVIR, NVIR, 2)
    x_other = lax.ppermute(x_send, "c", ring(2, 1))
    x = [jnp.stack([x_own, x_other])]
    x = x + [lax.ppermute(x[0], "z", ring(4, s)) for s in (1, 2, 3)]
    acc, x2 = early(where, x, own, other)
    acc = late(where, x2, own, other, acc)
    parts = lax.all_to_all(acc, MOST, 0, 0, tiled=True)
    part = jnp.sum(parts.reshape(NCHIP, 2, 4, HALF, NVIR).astype(F32), (0, 2)).astype(BF16)
    part = jnp.broadcast_to(part.reshape(1, NVEC, NVIR), (8, NVEC, NVIR))
    every = lax.all_to_all(part, NARROW, 0, 0, tiled=True)
    total = jnp.sum(every.reshape(2, OCC_DEV, NVEC, NVIR).astype(F32), 0)
    total = total.transpose(1, 0, 2).reshape(NVEC, PAIRS)
    w = lax.axis_index(WIDE)
    occ = lax.dynamic_slice_in_dim(occ_energy, w * OCC_DEV, OCC_DEV)
    delta = (vir_energy[None, :] - occ[:, None]).reshape(PAIRS)
    return delta[None, :] * trials.astype(F32) - total


def solution(mesh):
    fine = Mesh(mesh.devices.reshape(4, 2, 2, 2, 4), ("x", "yl", "c", "yh", "z"))
    in_specs = (P(NARROW, WIDE), P(None, WIDE), P(), P())
    return jax.shard_map(body, mesh=fine, in_specs=in_specs, out_specs=P(None, WIDE), check_vma=False)
```

```python
import jax
import jax.numpy as jnp
from jax import lax
from jax.experimental import pallas as pl
from jax.experimental.pallas import tpu as pltpu
from jax.sharding import Mesh, PartitionSpec as P

NOCC = 64
NVIR = 768
NVEC = 32
NCHIP = 8
OCC_DEV = 4
PAIRS = OCC_DEV * NVIR
HALF = 16
CHUNKS = 3
ROWS = NOCC * HALF

F32 = jnp.float32
BF16 = jnp.bfloat16

CHIPS = ("x", "yl")
WIDE = ("x", "yl", "c")
NARROW = ("yh", "z")
MOST = ("x", "yl", "c", "z")


def swap_blocks(tile):
    v = [tile[j * 16 : (j + 1) * 16] for j in range(8)]
    lane = lax.broadcasted_iota(jnp.int32, (16, 128), 1)
    for s in (4, 2, 1):
        bit = (lane & (16 * s)) != 0
        new = list(v)
        for j in range(8):
            if j & s:
                continue
            lo, hi = v[j], v[j + s]
            new[j] = jnp.where(bit, pltpu.roll(hi, 16 * s, 1), lo)
            new[j + s] = jnp.where(bit, hi, pltpu.roll(lo, 128 - 16 * s, 1))
        v = new
    return jnp.concatenate(v, 0)


def fetch_rows(b2, own, other, sems):
    copies = []
    for rel, src in enumerate((own, other)):
        for q in range(OCC_DEV):
            there = b2.at[pl.ds(rel * NCHIP, NCHIP), q]
            cp = pltpu.make_async_copy(src.at[:, :, pl.ds(q * NVIR, NVIR)], there, sems.at[rel * OCC_DEV + q])
            cp.start()
            copies.append(cp)
    return copies


def rows_of(ref, start, count):
    return ref[start // 64 : (start + count) // 64].reshape(count, NVIR)


def contract_first(x2, b2, d, copies):
    row_i = lax.broadcasted_iota(jnp.int32, (128, 128), 0) // 16
    lane_i = lax.broadcasted_iota(jnp.int32, (128, 128), 1) // 16
    diag = row_i == lane_i
    fit = jnp.zeros((128, 128), F32)
    for g in range(4):
        if g % 2 == 0:
            for cp in copies[g * 2 : g * 2 + 4]:
                cp.wait()
        rhs = rows_of(b2, g * 256, 256)
        for rb in range(4):
            lhs = rows_of(x2, rb * 256, 256)
            inter = lax.dot_general(lhs, rhs, (((1,), (1,)), ((), ())), preferred_element_type=F32)
            for a in range(2):
                for h in range(2):
                    ig, jg = g * 2 + h, rb * 2 + a
                    tile = inter[a * 128 : (a + 1) * 128, h * 128 : (h + 1) * 128]
                    if ig == jg:
                        fit = fit + jnp.where(diag, tile, 0.0)
                    d[ig * 128 : (ig + 1) * 128, jg * 128 : (jg + 1) * 128] = swap_blocks(tile).astype(BF16)
    total = fit[0:16, :]
    for j in range(1, 8):
        total = total + fit[j * 16 : (j + 1) * 16, :]
    for s in (64, 32, 16):
        total = total + pltpu.roll(total, s, 1)
    fit_b = 2.0 * total.astype(BF16).astype(F32)
    sub = jnp.where(diag, jnp.concatenate([fit_b] * 8, 0), 0.0)
    for g in range(8):
        s = slice(g * 128, (g + 1) * 128)
        d[s, s] = (d[s, s].astype(F32) - sub).astype(BF16)


def early_kernel(where, x_a, x_b, x_c, x_d, own0, other0, own1, other1, out, x_out, x2, b_a, b_b, d, acc, xs, bs, os):
    z = where[1]
    gets = []
    for s, ref in enumerate((x_a, x_b, x_c, x_d)):
        gets.append(pltpu.make_async_copy(ref, x2.at[:, (z - s) & 3], xs.at[s]))
        gets[-1].start()
    rows0 = fetch_rows(b_a, own0, other0, bs.at[0])
    rows1 = fetch_rows(b_b, own1, other1, bs.at[1])
    for cp in gets:
        cp.wait()
    keep_x = pltpu.make_async_copy(x2, x_out, xs.at[4])
    keep_x.start()
    puts = []
    for t, (b2, copies) in enumerate(((b_a, rows0), (b_b, rows1))):
        contract_first(x2, b2, d, copies)
        for rb in range(4):
            rows = slice(rb * 256, (rb + 1) * 256)
            term = jnp.dot(d[rows, :], rows_of(b2, 0, ROWS), preferred_element_type=F32)
            if t == 0:
                acc[rows, :] = term
            else:
                acc[rows, :] += term
                puts.append(pltpu.make_async_copy(acc.at[rows], out.at[rows], os.at[rb]))
                puts[-1].start()
    keep_x.wait()
    for cp in puts:
        cp.wait()


def late_kernel(where, x_in, own, other, acc_in, out, x2, b2, d, acc, res, xs, bs, os):
    c = where[0]
    get_x = pltpu.make_async_copy(x_in, x2, xs.at[0])
    get_x.start()
    copies = fetch_rows(b2, own, other, bs)
    get_acc = pltpu.make_async_copy(acc_in, acc, xs.at[1])
    get_acc.start()
    get_x.wait()
    contract_first(x2, b2, d, copies)
    get_acc.wait()
    puts = []
    for rb in range(4):
        rows = slice(rb * 256, (rb + 1) * 256)
        term = acc[rows, :] + jnp.dot(d[rows, :], rows_of(b2, 0, ROWS), preferred_element_type=F32)
        res[rb * 4 : (rb + 1) * 4] = term.astype(BF16).reshape(4, OCC_DEV, HALF, NVIR)
        for k in range(4):
            rel, chip = rb // 2, (rb % 2) * 4 + k
            puts.append(pltpu.make_async_copy(res.at[rb * 4 + k], out.at[chip * 2 + (c ^ rel)], os.at[rb * 4 + k]))
            puts[-1].start()
    for cp in puts:
        cp.wait()


SMEM = pl.BlockSpec(memory_space=pltpu.SMEM)
ANY = pl.BlockSpec(memory_space=pl.ANY)
BLOCK = (16, OCC_DEV, HALF, NVIR)


def cost(count):
    return pl.CostEstimate(flops=count * 4 * ROWS * ROWS * NVIR, bytes_accessed=4 * ROWS * NVIR * 2, transcendentals=0)


def early(where, x, own, other):
    return pl.pallas_call(
        early_kernel,
        out_shape=[jax.ShapeDtypeStruct((ROWS, NVIR), F32), jax.ShapeDtypeStruct(BLOCK, BF16)],
        in_specs=[SMEM] + [ANY] * 8,
        out_specs=[ANY, ANY],
        scratch_shapes=[
            pltpu.VMEM(BLOCK, BF16),
            pltpu.VMEM(BLOCK, BF16),
            pltpu.VMEM(BLOCK, BF16),
            pltpu.VMEM((ROWS, ROWS), BF16),
            pltpu.VMEM((ROWS, NVIR), F32),
            pltpu.SemaphoreType.DMA((5,)),
            pltpu.SemaphoreType.DMA((2, 8)),
            pltpu.SemaphoreType.DMA((4,)),
        ],
        cost_estimate=cost(2),
        compiler_params=pltpu.CompilerParams(vmem_limit_bytes=60 << 20),
        name="terms_early",
    )(where, *x, own[0], other[0], own[1], other[1])


def late(where, x2, own, other, acc):
    return pl.pallas_call(
        late_kernel,
        out_shape=jax.ShapeDtypeStruct(BLOCK, BF16),
        in_specs=[SMEM] + [ANY] * 4,
        out_specs=ANY,
        scratch_shapes=[
            pltpu.VMEM(BLOCK, BF16),
            pltpu.VMEM(BLOCK, BF16),
            pltpu.VMEM((ROWS, ROWS), BF16),
            pltpu.VMEM((ROWS, NVIR), F32),
            pltpu.VMEM(BLOCK, BF16),
            pltpu.SemaphoreType.DMA((2,)),
            pltpu.SemaphoreType.DMA((8,)),
            pltpu.SemaphoreType.DMA((16,)),
        ],
        cost_estimate=cost(1),
        compiler_params=pltpu.CompilerParams(vmem_limit_bytes=60 << 20),
        name="terms_late",
    )(where, x2, own[2], other[2], acc).reshape(16 * OCC_DEV, HALF, NVIR)


def ring(n, s):
    return [(i, (i + s) % n) for i in range(n)]


def body(fit_rows, trials, occ_energy, vir_energy):
    core = lax.axis_index("c").astype(jnp.int32)
    z = lax.axis_index("z").astype(jnp.int32)
    where = jnp.stack([core, z])
    blocks = [fit_rows.reshape(CHUNKS, NCHIP, HALF, PAIRS)]
    for _ in range(1, CHUNKS):
        blocks.append(lax.optimization_barrier(blocks[-1]))
    mine = lax.dynamic_slice_in_dim(trials, z * NVIR, NVIR, 1)
    mine = jnp.concatenate([mine[:HALF], mine[HALF:]], 1)
    mine = jnp.broadcast_to(mine[None], (NCHIP, HALF, 2 * NVIR))
    own, other = [], []
    for t in range(CHUNKS):
        send = blocks[t][t]
        if t == 0:
            send = jnp.concatenate([send, mine], 2)
        own.append(lax.all_to_all(send, CHIPS, 0, 0, tiled=True))
        other.append(lax.ppermute(own[t], "c", ring(2, 1)))
    x_own = lax.dynamic_slice_in_dim(own[0], PAIRS + core * NVIR, NVIR, 2)
    x_send = lax.dynamic_slice_in_dim(own[0], PAIRS + (1 - core) * NVIR, NVIR, 2)
    x_other = lax.ppermute(x_send, "c", ring(2, 1))
    x = [jnp.concatenate([x_own, x_other])]
    x = x + [lax.ppermute(x[0], "z", ring(4, s)) for s in (1, 2, 3)]
    acc, x2 = early(where, x, own, other)
    acc = late(where, x2, own, other, acc)
    parts = lax.all_to_all(acc, MOST, 0, 0, tiled=True)
    part = jnp.sum(parts.reshape(NCHIP, 2, 4, HALF, NVIR).astype(F32), (0, 2)).astype(BF16)
    part = jnp.broadcast_to(part.reshape(1, NVEC, NVIR), (8, NVEC, NVIR))
    every = lax.all_to_all(part, NARROW, 0, 0, tiled=True)
    total = jnp.sum(every.reshape(2, OCC_DEV, NVEC, NVIR).astype(F32), 0)
    total = total.transpose(1, 0, 2).reshape(NVEC, PAIRS)
    w = lax.axis_index(WIDE)
    occ = lax.dynamic_slice_in_dim(occ_energy, w * OCC_DEV, OCC_DEV)
    delta = (vir_energy[None, :] - occ[:, None]).reshape(PAIRS)
    return delta[None, :] * trials.astype(F32) - total


def solution(mesh):
    fine = Mesh(mesh.devices.reshape(4, 2, 2, 2, 4), ("x", "yl", "c", "yh", "z"))
    in_specs = (P(NARROW, WIDE), P(None, WIDE), P(), P())
    return jax.shard_map(body, mesh=fine, in_specs=in_specs, out_specs=P(None, WIDE), check_vma=False)
```

```python
import jax
import jax.numpy as jnp
from jax import lax
from jax.experimental import pallas as pl
from jax.experimental.pallas import tpu as pltpu
from jax.sharding import Mesh, PartitionSpec as P

NOCC = 64
NVIR = 768
NVEC = 32
NCHIP = 8
OCC_DEV = 4
PAIRS = OCC_DEV * NVIR
HALF = 16
CHUNKS = 3
ROWS = NOCC * HALF

F32 = jnp.float32
BF16 = jnp.bfloat16

CHIPS = ("x", "yl")
WIDE = ("x", "yl", "c")
NARROW = ("yh", "z")
MOST = ("x", "yl", "c", "z")


def swap_blocks(tile):
    v = [tile[j * 16 : (j + 1) * 16] for j in range(8)]
    lane = lax.broadcasted_iota(jnp.int32, (16, 128), 1)
    for s in (4, 2, 1):
        bit = (lane & (16 * s)) != 0
        new = list(v)
        for j in range(8):
            if j & s:
                continue
            lo, hi = v[j], v[j + s]
            new[j] = jnp.where(bit, pltpu.roll(hi, 16 * s, 1), lo)
            new[j + s] = jnp.where(bit, hi, pltpu.roll(lo, 128 - 16 * s, 1))
        v = new
    return jnp.concatenate(v, 0)


def fetch_rows(b2, own, other, sems):
    copies = []
    for rel, src in enumerate((own, other)):
        for q in range(OCC_DEV):
            there = b2.at[pl.ds(rel * NCHIP, NCHIP), q]
            cp = pltpu.make_async_copy(src.at[:, :, pl.ds(q * NVIR, NVIR)], there, sems.at[rel * OCC_DEV + q])
            cp.start()
            copies.append(cp)
    return copies


def rows_of(ref, start, count):
    return ref[start // 64 : (start + count) // 64].reshape(count, NVIR)


def contract_first(x2, b2, d, diag, copies):
    for g in range(4):
        if g % 2 == 0:
            for cp in copies[g * 2 : g * 2 + 4]:
                cp.wait()
        rhs = rows_of(b2, g * 256, 256)
        for rb in range(4):
            lhs = rows_of(x2, rb * 256, 256)
            inter = lax.dot_general(lhs, rhs, (((1,), (1,)), ((), ())), preferred_element_type=F32)
            for a in range(2):
                for h in range(2):
                    ig, jg = g * 2 + h, rb * 2 + a
                    tile = inter[a * 128 : (a + 1) * 128, h * 128 : (h + 1) * 128]
                    if ig == jg:
                        diag[ig] = tile
                    d[ig * 128 : (ig + 1) * 128, jg * 128 : (jg + 1) * 128] = swap_blocks(tile).astype(BF16)
    same = lax.broadcasted_iota(jnp.int32, (128, 128), 0) // 16 == lax.broadcasted_iota(jnp.int32, (128, 128), 1) // 16
    fit = diag[0]
    for k in range(1, 8):
        fit = fit + diag[k]
    fit = jnp.where(same, fit, 0.0)
    total = fit[0:16, :]
    for j in range(1, 8):
        total = total + fit[j * 16 : (j + 1) * 16, :]
    for s in (64, 32, 16):
        total = total + pltpu.roll(total, s, 1)
    double = 2.0 * total.astype(BF16).astype(F32)
    return jnp.where(same, jnp.concatenate([double] * 8, 0), 0.0).astype(BF16)


def contract_second(b2, d, acc, clear):
    for rb in range(4):
        rows = slice(rb * 256, (rb + 1) * 256)
        term = jnp.dot(d[rows, :], rows_of(b2, 0, ROWS), preferred_element_type=F32)
        acc[rows, :] = term if clear else acc[rows, :] + term


def early_kernel(where, x_a, x_b, x_c, x_d, own0, other0, own1, other1, out, x_out, x2, b_a, b_b, d, acc, diag, xs, bs, os):
    z = where[1]
    gets = []
    for s, ref in enumerate((x_a, x_b, x_c, x_d)):
        gets.append(pltpu.make_async_copy(ref, x2.at[:, (z - s) & 3], xs.at[s]))
        gets[-1].start()
    rows0 = fetch_rows(b_a, own0, other0, bs.at[0])
    rows1 = fetch_rows(b_b, own1, other1, bs.at[1])
    for cp in gets:
        cp.wait()
    keep_x = pltpu.make_async_copy(x2, x_out, xs.at[4])
    keep_x.start()
    puts = []
    for t, (b2, copies) in enumerate(((b_a, rows0), (b_b, rows1))):
        fit = contract_first(x2, b2, d, diag, copies)
        contract_second(b2, d, acc, t == 0)
        for g in range(8):
            rows = slice(g * 128, (g + 1) * 128)
            acc[rows, :] -= jnp.dot(fit, rows_of(b2, g * 128, 128), preferred_element_type=F32)
            if t == 1:
                puts.append(pltpu.make_async_copy(acc.at[rows], out.at[rows], os.at[g]))
                puts[-1].start()
    keep_x.wait()
    for cp in puts:
        cp.wait()


def late_kernel(where, x_in, own, other, acc_in, out, x2, b2, d, acc, diag, res, xs, bs, os):
    c = where[0]
    get_x = pltpu.make_async_copy(x_in, x2, xs.at[0])
    get_x.start()
    copies = fetch_rows(b2, own, other, bs)
    get_acc = pltpu.make_async_copy(acc_in, acc, xs.at[1])
    get_acc.start()
    get_x.wait()
    fit = contract_first(x2, b2, d, diag, copies)
    get_acc.wait()
    contract_second(b2, d, acc, False)
    puts = []
    for g in range(8):
        term = acc[g * 128 : (g + 1) * 128, :] - jnp.dot(fit, rows_of(b2, g * 128, 128), preferred_element_type=F32)
        res[g * 2 : (g + 1) * 2] = term.astype(BF16).reshape(2, OCC_DEV, HALF, NVIR)
        for k in range(2):
            rel, chip = g // 4, (g % 4) * 2 + k
            puts.append(pltpu.make_async_copy(res.at[g * 2 + k], out.at[chip * 2 + (c ^ rel)], os.at[g * 2 + k]))
            puts[-1].start()
    for cp in puts:
        cp.wait()


SMEM = pl.BlockSpec(memory_space=pltpu.SMEM)
ANY = pl.BlockSpec(memory_space=pl.ANY)
BLOCK = (16, OCC_DEV, HALF, NVIR)


def cost(count):
    return pl.CostEstimate(flops=count * 4 * ROWS * ROWS * NVIR, bytes_accessed=4 * ROWS * NVIR * 2, transcendentals=0)


def early(where, x, own, other):
    return pl.pallas_call(
        early_kernel,
        out_shape=[jax.ShapeDtypeStruct((ROWS, NVIR), F32), jax.ShapeDtypeStruct(BLOCK, BF16)],
        in_specs=[SMEM] + [ANY] * 8,
        out_specs=[ANY, ANY],
        scratch_shapes=[
            pltpu.VMEM(BLOCK, BF16),
            pltpu.VMEM(BLOCK, BF16),
            pltpu.VMEM(BLOCK, BF16),
            pltpu.VMEM((ROWS, ROWS), BF16),
            pltpu.VMEM((ROWS, NVIR), F32),
            pltpu.VMEM((8, 128, 128), F32),
            pltpu.SemaphoreType.DMA((5,)),
            pltpu.SemaphoreType.DMA((2, 8)),
            pltpu.SemaphoreType.DMA((8,)),
        ],
        cost_estimate=cost(2),
        compiler_params=pltpu.CompilerParams(vmem_limit_bytes=60 << 20),
        name="terms_early",
    )(where, *x, own[0], other[0], own[1], other[1])


def late(where, x2, own, other, acc):
    return pl.pallas_call(
        late_kernel,
        out_shape=jax.ShapeDtypeStruct(BLOCK, BF16),
        in_specs=[SMEM] + [ANY] * 4,
        out_specs=ANY,
        scratch_shapes=[
            pltpu.VMEM(BLOCK, BF16),
            pltpu.VMEM(BLOCK, BF16),
            pltpu.VMEM((ROWS, ROWS), BF16),
            pltpu.VMEM((ROWS, NVIR), F32),
            pltpu.VMEM((8, 128, 128), F32),
            pltpu.VMEM(BLOCK, BF16),
            pltpu.SemaphoreType.DMA((2,)),
            pltpu.SemaphoreType.DMA((8,)),
            pltpu.SemaphoreType.DMA((16,)),
        ],
        cost_estimate=cost(1),
        compiler_params=pltpu.CompilerParams(vmem_limit_bytes=60 << 20),
        name="terms_late",
    )(where, x2, own[2], other[2], acc).reshape(16 * OCC_DEV, HALF, NVIR)


def ring(n, s):
    return [(i, (i + s) % n) for i in range(n)]


def body(fit_rows, trials, occ_energy, vir_energy):
    core = lax.axis_index("c").astype(jnp.int32)
    z = lax.axis_index("z").astype(jnp.int32)
    where = jnp.stack([core, z])
    blocks = [fit_rows.reshape(CHUNKS, NCHIP, HALF, PAIRS)]
    for _ in range(1, CHUNKS):
        blocks.append(lax.optimization_barrier(blocks[-1]))
    mine = lax.dynamic_slice_in_dim(trials, z * NVIR, NVIR, 1)
    mine = jnp.concatenate([mine[:HALF], mine[HALF:]], 1)
    mine = jnp.broadcast_to(mine[None], (NCHIP, HALF, 2 * NVIR))
    own, other = [], []
    for t in range(CHUNKS):
        send = blocks[t][t]
        if t == 0:
            send = jnp.concatenate([send, mine], 2)
        own.append(lax.all_to_all(send, CHIPS, 0, 0, tiled=True))
        other.append(lax.ppermute(own[t], "c", ring(2, 1)))
    x_own = lax.dynamic_slice_in_dim(own[0], PAIRS + core * NVIR, NVIR, 2)
    x_send = lax.dynamic_slice_in_dim(own[0], PAIRS + (1 - core) * NVIR, NVIR, 2)
    x_other = lax.ppermute(x_send, "c", ring(2, 1))
    x = [jnp.concatenate([x_own, x_other])]
    x = x + [lax.ppermute(x[0], "z", ring(4, s)) for s in (1, 2, 3)]
    acc, x2 = early(where, x, own, other)
    acc = late(where, x2, own, other, acc)
    parts = lax.all_to_all(acc, MOST, 0, 0, tiled=True)
    part = jnp.sum(parts.reshape(NCHIP, 2, 4, HALF, NVIR).astype(F32), (0, 2)).astype(BF16)
    part = jnp.broadcast_to(part.reshape(1, NVEC, NVIR), (8, NVEC, NVIR))
    every = lax.all_to_all(part, NARROW, 0, 0, tiled=True)
    total = jnp.sum(every.reshape(2, OCC_DEV, NVEC, NVIR).astype(F32), 0)
    total = total.transpose(1, 0, 2).reshape(NVEC, PAIRS)
    w = lax.axis_index(WIDE)
    occ = lax.dynamic_slice_in_dim(occ_energy, w * OCC_DEV, OCC_DEV)
    delta = (vir_energy[None, :] - occ[:, None]).reshape(PAIRS)
    return delta[None, :] * trials.astype(F32) - total


def solution(mesh):
    fine = Mesh(mesh.devices.reshape(4, 2, 2, 2, 4), ("x", "yl", "c", "yh", "z"))
    in_specs = (P(NARROW, WIDE), P(None, WIDE), P(), P())
    return jax.shard_map(body, mesh=fine, in_specs=in_specs, out_specs=P(None, WIDE), check_vma=False)
```

```python
import jax
import jax.numpy as jnp
from jax import lax
from jax.experimental import pallas as pl
from jax.experimental.pallas import tpu as pltpu
from jax.sharding import Mesh, PartitionSpec as P

NOCC = 64
NVIR = 768
NVEC = 32
NCHIP = 8
OCC_DEV = 4
PAIRS = OCC_DEV * NVIR
HALF = 16
CHUNKS = 3
ROWS = NOCC * HALF

F32 = jnp.float32
BF16 = jnp.bfloat16

CHIPS = ("x", "yl")
WIDE = ("x", "yl", "c")
NARROW = ("yh", "z")
MOST = ("x", "yl", "c", "z")


def swap_blocks(tile):
    v = [tile[j * 16 : (j + 1) * 16] for j in range(8)]
    lane = lax.broadcasted_iota(jnp.int32, (16, 128), 1)
    for s in (4, 2, 1):
        bit = (lane & (16 * s)) != 0
        new = list(v)
        for j in range(8):
            if j & s:
                continue
            lo, hi = v[j], v[j + s]
            new[j] = jnp.where(bit, pltpu.roll(hi, 16 * s, 1), lo)
            new[j + s] = jnp.where(bit, hi, pltpu.roll(lo, 128 - 16 * s, 1))
        v = new
    return jnp.concatenate(v, 0)


def fetch_rows(b2, own, other, sems):
    copies = []
    for rel, src in enumerate((own, other)):
        for q in range(OCC_DEV):
            there = b2.at[pl.ds(rel * NCHIP, NCHIP), q]
            cp = pltpu.make_async_copy(src.at[:, :, pl.ds(q * NVIR, NVIR)], there, sems.at[rel * OCC_DEV + q])
            cp.start()
            copies.append(cp)
    return copies


def rows_of(ref, start, count):
    return ref[start // 64 : (start + count) // 64].reshape(count, NVIR)


def contract_first(x2, b2, d, diag, gets, copies):
    for g in range(4):
        if g % 2 == 0:
            for cp in copies[g * 2 : g * 2 + 4]:
                cp.wait()
        rhs = rows_of(b2, g * 256, 256)
        for rb in range(4):
            if g == 0 and gets:
                gets[rb].wait()
            lhs = rows_of(x2, rb * 256, 256)
            inter = lax.dot_general(lhs, rhs, (((1,), (1,)), ((), ())), preferred_element_type=F32)
            for a in range(2):
                for h in range(2):
                    ig, jg = g * 2 + h, rb * 2 + a
                    tile = inter[a * 128 : (a + 1) * 128, h * 128 : (h + 1) * 128]
                    if ig == jg:
                        diag[ig] = tile
                    d[ig * 128 : (ig + 1) * 128, jg * 128 : (jg + 1) * 128] = swap_blocks(tile).astype(BF16)
    same = lax.broadcasted_iota(jnp.int32, (128, 128), 0) // 16 == lax.broadcasted_iota(jnp.int32, (128, 128), 1) // 16
    fit = diag[0]
    for k in range(1, 8):
        fit = fit + diag[k]
    fit = jnp.where(same, fit, 0.0)
    total = fit[0:16, :]
    for j in range(1, 8):
        total = total + fit[j * 16 : (j + 1) * 16, :]
    for s in (64, 32, 16):
        total = total + pltpu.roll(total, s, 1)
    double = 2.0 * total.astype(BF16).astype(F32)
    return jnp.where(same, jnp.concatenate([double] * 8, 0), 0.0).astype(BF16)


def contract_second(b2, d, acc, clear):
    for rb in range(4):
        rows = slice(rb * 256, (rb + 1) * 256)
        term = jnp.dot(d[rows, :], rows_of(b2, 0, ROWS), preferred_element_type=F32)
        acc[rows, :] = term if clear else acc[rows, :] + term


def early_kernel(where, x_a, x_b, x_c, x_d, own0, other0, own1, other1, out, x_out, x2, b_a, b_b, d, acc, diag, xs, bs, os):
    z = where[1]
    gets = []
    for s, ref in enumerate((x_a, x_b, x_c, x_d)):
        gets.append(pltpu.make_async_copy(ref, x2.at[:, (z - s) & 3], xs.at[s]))
        gets[-1].start()
    rows0 = fetch_rows(b_a, own0, other0, bs.at[0])
    rows1 = fetch_rows(b_b, own1, other1, bs.at[1])
    for cp in gets:
        cp.wait()
    keep_x = pltpu.make_async_copy(x2, x_out, xs.at[4])
    keep_x.start()
    puts = []
    for t, (b2, copies) in enumerate(((b_a, rows0), (b_b, rows1))):
        fit = contract_first(x2, b2, d, diag, [], copies)
        contract_second(b2, d, acc, t == 0)
        for g in range(8):
            rows = slice(g * 128, (g + 1) * 128)
            acc[rows, :] -= jnp.dot(fit, rows_of(b2, g * 128, 128), preferred_element_type=F32)
            if t == 1:
                puts.append(pltpu.make_async_copy(acc.at[rows], out.at[rows], os.at[g]))
                puts[-1].start()
    keep_x.wait()
    for cp in puts:
        cp.wait()


def late_kernel(where, x_in, own, other, acc_in, out, x2, b2, d, acc, diag, xs, os):
    c = where[0]
    gets = []
    for k in range(4):
        gets.append(pltpu.make_async_copy(x_in.at[pl.ds(k * 4, 4)], x2.at[pl.ds(k * 4, 4)], xs.at[k]))
        gets[-1].start()
    get_acc = pltpu.make_async_copy(acc_in, acc, os.at[0])
    get_acc.start()
    for rel, src in enumerate((own, other)):
        for chip in range(NCHIP):
            for q in range(OCC_DEV):
                b2[rel * NCHIP + chip, q] = src[chip, :, q * NVIR : (q + 1) * NVIR]
    fit = contract_first(x2, b2, d, diag, gets, [])
    get_acc.wait()
    contract_second(b2, d, acc, False)
    for g in range(8):
        term = acc[g * 128 : (g + 1) * 128, :] - jnp.dot(fit, rows_of(b2, g * 128, 128), preferred_element_type=F32)
        term = term.astype(BF16).reshape(2, OCC_DEV, HALF, NVIR)
        for k in range(2):
            rel, chip = g // 4, (g % 4) * 2 + k
            out[chip * 2 + (c ^ rel)] = term[k]


VMEM = pl.BlockSpec(memory_space=pltpu.VMEM)
LATE_MIB = 50
SMEM = pl.BlockSpec(memory_space=pltpu.SMEM)
ANY = pl.BlockSpec(memory_space=pl.ANY)
BLOCK = (16, OCC_DEV, HALF, NVIR)


def cost(count):
    return pl.CostEstimate(flops=count * 4 * ROWS * ROWS * NVIR, bytes_accessed=4 * ROWS * NVIR * 2, transcendentals=0)


def early(where, x, own, other):
    return pl.pallas_call(
        early_kernel,
        out_shape=[jax.ShapeDtypeStruct((ROWS, NVIR), F32), jax.ShapeDtypeStruct(BLOCK, BF16)],
        in_specs=[SMEM] + [ANY] * 8,
        out_specs=[ANY, ANY],
        scratch_shapes=[
            pltpu.VMEM(BLOCK, BF16),
            pltpu.VMEM(BLOCK, BF16),
            pltpu.VMEM(BLOCK, BF16),
            pltpu.VMEM((ROWS, ROWS), BF16),
            pltpu.VMEM((ROWS, NVIR), F32),
            pltpu.VMEM((8, 128, 128), F32),
            pltpu.SemaphoreType.DMA((5,)),
            pltpu.SemaphoreType.DMA((2, 8)),
            pltpu.SemaphoreType.DMA((8,)),
        ],
        cost_estimate=cost(2),
        compiler_params=pltpu.CompilerParams(vmem_limit_bytes=60 << 20),
        name="terms_early",
    )(where, *x, own[0], other[0], own[1], other[1])


def late(where, x2, own, other, acc):
    return pl.pallas_call(
        late_kernel,
        out_shape=jax.ShapeDtypeStruct(BLOCK, BF16),
        in_specs=[SMEM, ANY, VMEM, VMEM, ANY],
        out_specs=VMEM,
        scratch_shapes=[
            pltpu.VMEM(BLOCK, BF16),
            pltpu.VMEM(BLOCK, BF16),
            pltpu.VMEM((ROWS, ROWS), BF16),
            pltpu.VMEM((ROWS, NVIR), F32),
            pltpu.VMEM((8, 128, 128), F32),
            pltpu.SemaphoreType.DMA((4,)),
            pltpu.SemaphoreType.DMA((1,)),
        ],
        cost_estimate=cost(1),
        compiler_params=pltpu.CompilerParams(vmem_limit_bytes=LATE_MIB << 20),
        name="terms_late",
    )(where, x2, own[2], other[2], acc).reshape(16 * OCC_DEV, HALF, NVIR)


def ring(n, s):
    return [(i, (i + s) % n) for i in range(n)]


def body(fit_rows, trials, occ_energy, vir_energy):
    core = lax.axis_index("c").astype(jnp.int32)
    z = (lax.axis_index("z") + 2 * lax.axis_index("yh")).astype(jnp.int32) & 3
    where = jnp.stack([core, z])
    blocks = [fit_rows.reshape(CHUNKS, NCHIP, HALF, PAIRS)]
    for _ in range(1, CHUNKS):
        blocks.append(lax.optimization_barrier(blocks[-1]))
    mine = lax.dynamic_slice_in_dim(trials, z * NVIR, NVIR, 1)
    mine = jnp.concatenate([mine[:HALF], mine[HALF:]], 1)
    mine = jnp.broadcast_to(mine[None], (NCHIP, HALF, 2 * NVIR))
    own, other = [], []
    for t in range(CHUNKS):
        send = blocks[t][t]
        if t == 0:
            send = jnp.concatenate([send, mine], 2)
        own.append(lax.all_to_all(send, CHIPS, 0, 0, tiled=True))
        other.append(lax.ppermute(own[t], "c", ring(2, 1)))
    x_own = lax.dynamic_slice_in_dim(own[0], PAIRS + core * NVIR, NVIR, 2)
    x_send = lax.dynamic_slice_in_dim(own[0], PAIRS + (1 - core) * NVIR, NVIR, 2)
    x_other = lax.ppermute(x_send, "c", ring(2, 1))
    x = [jnp.concatenate([x_own, x_other])]
    steps = (("z", ring(4, 1)), ("yh", ring(2, 1)), ("z", ring(4, 3)))
    x = x + [lax.ppermute(x[0], axis, perm) for axis, perm in steps]
    acc, x2 = early(where, x, own, other)
    acc = late(where, x2, own, other, acc)
    parts = lax.all_to_all(acc, MOST, 0, 0, tiled=True)
    part = jnp.sum(parts.reshape(NCHIP, 2, 4, HALF, NVIR).astype(F32), (0, 2)).astype(BF16)
    part = jnp.broadcast_to(part.reshape(1, NVEC, NVIR), (8, NVEC, NVIR))
    every = lax.all_to_all(part, NARROW, 0, 0, tiled=True)
    total = jnp.sum(every.reshape(2, OCC_DEV, NVEC, NVIR).astype(F32), 0)
    total = total.transpose(1, 0, 2).reshape(NVEC, PAIRS)
    w = lax.axis_index(WIDE)
    occ = lax.dynamic_slice_in_dim(occ_energy, w * OCC_DEV, OCC_DEV)
    delta = (vir_energy[None, :] - occ[:, None]).reshape(PAIRS)
    return delta[None, :] * trials.astype(F32) - total


def solution(mesh):
    fine = Mesh(mesh.devices.reshape(4, 2, 2, 2, 4), ("x", "yl", "c", "yh", "z"))
    in_specs = (P(NARROW, WIDE), P(None, WIDE), P(), P())
    return jax.shard_map(body, mesh=fine, in_specs=in_specs, out_specs=P(None, WIDE), check_vma=False)
```

```python
import jax
import jax.numpy as jnp
from jax import lax
from jax.experimental import pallas as pl
from jax.experimental.pallas import tpu as pltpu
from jax.sharding import Mesh, PartitionSpec as P

NOCC = 64
NVIR = 768
NVEC = 32
NCHIP = 8
OCC_DEV = 4
PAIRS = OCC_DEV * NVIR
HALF = 16
CHUNKS = 3
ROWS = NOCC * HALF

F32 = jnp.float32
BF16 = jnp.bfloat16

CHIPS = ("x", "yl")
WIDE = ("x", "yl", "c")
NARROW = ("yh", "z")
MOST = ("x", "yl", "c", "z")


def swap_blocks(tile):
    v = [tile[j * 16 : (j + 1) * 16] for j in range(8)]
    lane = lax.broadcasted_iota(jnp.int32, (16, 128), 1)
    for s in (4, 2, 1):
        bit = (lane & (16 * s)) != 0
        new = list(v)
        for j in range(8):
            if j & s:
                continue
            lo, hi = v[j], v[j + s]
            new[j] = jnp.where(bit, pltpu.roll(hi, 16 * s, 1), lo)
            new[j + s] = jnp.where(bit, hi, pltpu.roll(lo, 128 - 16 * s, 1))
        v = new
    return jnp.concatenate(v, 0)


def rows_of(ref, start, count):
    return ref[start // 64 : (start + count) // 64].reshape(count, NVIR)


def get_rows(b2, own, other, g, sems):
    src, chips = (own, other)[g // 2], pl.ds((g % 2) * 4, 4)
    copies = []
    for q in range(OCC_DEV):
        lanes = pl.ds(q * NVIR, NVIR)
        copies.append(pltpu.make_async_copy(src.at[chips, :, lanes], b2.at[pl.ds(g * 4, 4), q], sems.at[g, q]))
    return copies


def contract_first(x2, b2, d, diag, order, before):
    for g, rb in order:
        before(g, rb)
        lhs, rhs = rows_of(x2, rb * 256, 256), rows_of(b2, g * 256, 256)
        inter = lax.dot_general(lhs, rhs, (((1,), (1,)), ((), ())), preferred_element_type=F32)
        for a in range(2):
            for h in range(2):
                ig, jg = g * 2 + h, rb * 2 + a
                tile = inter[a * 128 : (a + 1) * 128, h * 128 : (h + 1) * 128]
                if ig == jg:
                    diag[ig] = tile
                d[ig * 128 : (ig + 1) * 128, jg * 128 : (jg + 1) * 128] = swap_blocks(tile).astype(BF16)
    same = lax.broadcasted_iota(jnp.int32, (128, 128), 0) // 16 == lax.broadcasted_iota(jnp.int32, (128, 128), 1) // 16
    fit = diag[0]
    for k in range(1, 8):
        fit = fit + diag[k]
    fit = jnp.where(same, fit, 0.0)
    total = fit[0:16, :]
    for j in range(1, 8):
        total = total + fit[j * 16 : (j + 1) * 16, :]
    for s in (64, 32, 16):
        total = total + pltpu.roll(total, s, 1)
    double = 2.0 * total.astype(BF16).astype(F32)
    return jnp.where(same, jnp.concatenate([double] * 8, 0), 0.0).astype(BF16)


def contract_second(b2, d, acc, fit, before, emit):
    def close(rb):
        for g in (rb * 2, rb * 2 + 1):
            rows = slice(g * 128, (g + 1) * 128)
            emit(g, acc[rows, :] - jnp.dot(fit, rows_of(b2, g * 128, 128), preferred_element_type=F32))

    for rb in range(4):
        rows = slice(rb * 256, (rb + 1) * 256)
        clear = before(rb)
        term = jnp.dot(d[rows, :], rows_of(b2, 0, ROWS), preferred_element_type=F32)
        acc[rows, :] = term if clear else acc[rows, :] + term
        if rb:
            close(rb - 1)
    close(3)


WAVE = sorted(((g, rb) for g in range(4) for rb in range(4)), key=lambda pair: (max(pair), pair))


def early_kernel(where, x_a, x_b, x_c, x_d, own0, other0, own1, other1, out, x_out, x2, b_a, b_b, d, acc, diag, xs, bs, os):
    z = where[1]
    gets, rows0, rows1 = [], [], []
    for k in range(4):
        part = pl.ds(k * 4, 4)
        gets.append([pltpu.make_async_copy(ref.at[part], x2.at[part, (z - s) & 3], xs.at[k, s]) for s, ref in enumerate((x_a, x_b, x_c, x_d))])
        rows0.append(get_rows(b_a, own0, other0, k, bs.at[0]))
        rows1.append(get_rows(b_b, own1, other1, k, bs.at[1]))
        for cp in gets[k] + rows0[k]:
            cp.start()
    keep_x = pltpu.make_async_copy(x2, x_out, xs.at[4, 0])
    puts = []

    def before0(g, rb):
        if max(g, rb) == g and rb == 0:
            for cp in rows0[g]:
                cp.wait()
        if g == 0:
            for cp in gets[rb]:
                cp.wait()
        if (g, rb) == WAVE[-1]:
            for row in rows1:
                for cp in row:
                    cp.start()

    def before1(g, rb):
        if rb == 0:
            for cp in rows1[g]:
                cp.wait()
        if (g, rb) == (1, 0):
            keep_x.start()

    def store(g, value):
        acc[g * 128 : (g + 1) * 128, :] = value

    def send(g, value):
        store(g, value)
        rows = pl.ds(g * 128, 128)
        puts.append(pltpu.make_async_copy(acc.at[rows], out.at[rows], os.at[g]))
        puts[-1].start()

    fit = contract_first(x2, b_a, d, diag, WAVE, before0)
    contract_second(b_a, d, acc, fit, lambda rb: True, store)
    fit = contract_first(x2, b_b, d, diag, [(g, rb) for g in range(4) for rb in range(4)], before1)
    contract_second(b_b, d, acc, fit, lambda rb: False, send)
    keep_x.wait()
    for cp in puts:
        cp.wait()


def late_kernel(where, x_in, own, other, acc_in, out, x2, b2, d, acc, diag, xs, os):
    c = where[0]
    gets, sums = [], []
    for k in range(4):
        part = pl.ds(k * 4, 4)
        gets.append(pltpu.make_async_copy(x_in.at[part], x2.at[part], xs.at[k]))
        gets[k].start()
        part = pl.ds(k * 256, 256)
        sums.append(pltpu.make_async_copy(acc_in.at[part], acc.at[part], os.at[k]))

    def before(g, rb):
        if g == 0:
            gets[rb].wait()
            if rb == 1:
                for cp in sums:
                    cp.start()
        if rb == 0:
            src = (own, other)[g // 2]
            for k in range(4):
                for q in range(OCC_DEV):
                    b2[g * 4 + k, q] = src[(g % 2) * 4 + k, :, q * NVIR : (q + 1) * NVIR]

    def before_sum(rb):
        sums[rb].wait()
        return False

    def emit(g, value):
        value = value.astype(BF16).reshape(2, OCC_DEV, HALF, NVIR)
        for k in range(2):
            rel, chip = g // 4, (g % 4) * 2 + k
            out[chip * 2 + (c ^ rel)] = value[k]

    fit = contract_first(x2, b2, d, diag, [(g, rb) for rb in range(4) for g in range(4)], before)
    contract_second(b2, d, acc, fit, before_sum, emit)


def final_kernel(where, occ, vir, trials, p_a, p_b, p_c, p_d, out):
    for s, ref in enumerate((p_a, p_b, p_c, p_d)):
        q = (where[0] - s) & 3
        lanes = pl.ds(pl.multiple_of(q * NVIR, NVIR), NVIR)
        delta = vir[...] - occ[where[1] * OCC_DEV + q]
        out[:, lanes] = delta * trials[:, lanes].astype(F32) - ref[...]


VMEM = pl.BlockSpec(memory_space=pltpu.VMEM)
LATE_MIB = 50
SMEM = pl.BlockSpec(memory_space=pltpu.SMEM)
ANY = pl.BlockSpec(memory_space=pl.ANY)
BLOCK = (16, OCC_DEV, HALF, NVIR)


def cost(count):
    return pl.CostEstimate(flops=count * 4 * ROWS * ROWS * NVIR, bytes_accessed=4 * ROWS * NVIR * 2, transcendentals=0)


def early(where, x, own, other):
    return pl.pallas_call(
        early_kernel,
        out_shape=[jax.ShapeDtypeStruct((ROWS, NVIR), F32), jax.ShapeDtypeStruct(BLOCK, BF16)],
        in_specs=[SMEM] + [ANY] * 8,
        out_specs=[ANY, ANY],
        scratch_shapes=[
            pltpu.VMEM(BLOCK, BF16),
            pltpu.VMEM(BLOCK, BF16),
            pltpu.VMEM(BLOCK, BF16),
            pltpu.VMEM((ROWS, ROWS), BF16),
            pltpu.VMEM((ROWS, NVIR), F32),
            pltpu.VMEM((8, 128, 128), F32),
            pltpu.SemaphoreType.DMA((5, 4)),
            pltpu.SemaphoreType.DMA((2, 4, 4)),
            pltpu.SemaphoreType.DMA((8,)),
        ],
        cost_estimate=cost(2),
        compiler_params=pltpu.CompilerParams(vmem_limit_bytes=60 << 20),
        name="terms_early",
    )(where, *x, own[0], other[0], own[1], other[1])


def late(where, x2, own, other, acc):
    return pl.pallas_call(
        late_kernel,
        out_shape=jax.ShapeDtypeStruct(BLOCK, BF16),
        in_specs=[SMEM, ANY, VMEM, VMEM, ANY],
        out_specs=VMEM,
        scratch_shapes=[
            pltpu.VMEM(BLOCK, BF16),
            pltpu.VMEM(BLOCK, BF16),
            pltpu.VMEM((ROWS, ROWS), BF16),
            pltpu.VMEM((ROWS, NVIR), F32),
            pltpu.VMEM((8, 128, 128), F32),
            pltpu.SemaphoreType.DMA((4,)),
            pltpu.SemaphoreType.DMA((4,)),
        ],
        cost_estimate=cost(1),
        compiler_params=pltpu.CompilerParams(vmem_limit_bytes=LATE_MIB << 20),
        name="terms_late",
    )(where, x2, own[2], other[2], acc).reshape(16 * OCC_DEV, HALF, NVIR)


def final(where, occ, vir, trials, pieces):
    return pl.pallas_call(
        final_kernel,
        out_shape=jax.ShapeDtypeStruct((NVEC, PAIRS), F32),
        in_specs=[SMEM, SMEM] + [VMEM] * 6,
        out_specs=VMEM,
        compiler_params=pltpu.CompilerParams(vmem_limit_bytes=16 << 20),
        name="final",
    )(where, occ, vir.reshape(1, NVIR), trials, *pieces)


def ring(n, s):
    return [(i, (i + s) % n) for i in range(n)]


def body(fit_rows, trials, occ_energy, vir_energy):
    core = lax.axis_index("c").astype(jnp.int32)
    z = (lax.axis_index("z") + 2 * lax.axis_index("yh")).astype(jnp.int32) & 3
    where = jnp.stack([core, z])
    blocks = [fit_rows.reshape(CHUNKS, NCHIP, HALF, PAIRS)]
    for _ in range(1, CHUNKS):
        blocks.append(lax.optimization_barrier(blocks[-1]))
    mine = lax.dynamic_slice_in_dim(trials, z * NVIR, NVIR, 1)
    mine = jnp.concatenate([mine[:HALF], mine[HALF:]], 1)
    mine = jnp.broadcast_to(mine[None], (NCHIP, HALF, 2 * NVIR))
    own, other = [], []
    for t in range(CHUNKS):
        send = blocks[t][t]
        if t == 0:
            send = jnp.concatenate([send, mine], 2)
        own.append(lax.all_to_all(send, CHIPS, 0, 0, tiled=True))
        other.append(lax.ppermute(own[t], "c", ring(2, 1)))
    x_own = lax.dynamic_slice_in_dim(own[0], PAIRS + core * NVIR, NVIR, 2)
    x_send = lax.dynamic_slice_in_dim(own[0], PAIRS + (1 - core) * NVIR, NVIR, 2)
    x_other = lax.ppermute(x_send, "c", ring(2, 1))
    x = [jnp.concatenate([x_own, x_other])]
    steps = (("z", ring(4, 1)), ("yh", ring(2, 1)), ("z", ring(4, 3)))
    x = x + [lax.ppermute(x[0], axis, perm) for axis, perm in steps]
    acc, x2 = early(where, x, own, other)
    acc = late(where, x2, own, other, acc)
    parts = lax.all_to_all(acc, MOST, 0, 0, tiled=True)
    part = jnp.sum(parts.reshape(NCHIP, 2, 4, HALF, NVIR).astype(F32), (0, 2)).reshape(NVEC, NVIR)
    part = part + lax.ppermute(part, "yh", ring(2, 1))
    pieces = [part] + [lax.ppermute(part, "z", ring(4, s)) for s in (1, 2, 3)]
    place = jnp.stack([lax.axis_index("z"), lax.axis_index(WIDE)]).astype(jnp.int32)
    return final(place, occ_energy, vir_energy, trials, pieces)


def solution(mesh):
    fine = Mesh(mesh.devices.reshape(4, 2, 2, 2, 4), ("x", "yl", "c", "yh", "z"))
    in_specs = (P(NARROW, WIDE), P(None, WIDE), P(), P())
    return jax.shard_map(body, mesh=fine, in_specs=in_specs, out_specs=P(None, WIDE), check_vma=False)
```

```python
import jax
import jax.numpy as jnp
from jax import lax
from jax.experimental import pallas as pl
from jax.experimental.pallas import tpu as pltpu
from jax.sharding import Mesh, PartitionSpec as P

NOCC = 64
NVIR = 768
NVEC = 32
NCHIP = 8
OCC_DEV = 4
PAIRS = OCC_DEV * NVIR
HALF = 16
STEPS = (1, 2)
ROWS = NOCC * HALF

F32 = jnp.float32
BF16 = jnp.bfloat16

CHIPS = ("x", "yl")
WIDE = ("x", "yl", "c")
NARROW = ("yh", "z")
MOST = ("x", "yl", "c", "z")


def swap_blocks(tile):
    v = [tile[j * 16 : (j + 1) * 16] for j in range(8)]
    lane = lax.broadcasted_iota(jnp.int32, (16, 128), 1)
    for s in (4, 2, 1):
        bit = (lane & (16 * s)) != 0
        new = list(v)
        for j in range(8):
            if j & s:
                continue
            lo, hi = v[j], v[j + s]
            new[j] = jnp.where(bit, pltpu.roll(hi, 16 * s, 1), lo)
            new[j + s] = jnp.where(bit, hi, pltpu.roll(lo, 128 - 16 * s, 1))
        v = new
    return jnp.concatenate(v, 0)


def rows_of(ref, start, count):
    return ref[start // 64 : (start + count) // 64].reshape(count, NVIR)


def take_rows(b2, own, other, step):
    for rel, src in enumerate((own, other)):
        for chip in range(NCHIP):
            for q in range(OCC_DEV):
                b2[rel * NCHIP + chip, q] = src[chip, step * HALF : (step + 1) * HALF, q * NVIR : (q + 1) * NVIR]


def contract_first(x2, b2, d, diag):
    for g, rb in ((g, rb) for g in range(4) for rb in range(4)):
        lhs, rhs = rows_of(x2, rb * 256, 256), rows_of(b2, g * 256, 256)
        inter = lax.dot_general(lhs, rhs, (((1,), (1,)), ((), ())), preferred_element_type=F32)
        for a in range(2):
            for h in range(2):
                ig, jg = g * 2 + h, rb * 2 + a
                tile = inter[a * 128 : (a + 1) * 128, h * 128 : (h + 1) * 128]
                if ig == jg:
                    diag[ig] = tile
                d[ig * 128 : (ig + 1) * 128, jg * 128 : (jg + 1) * 128] = swap_blocks(tile).astype(BF16)
    same = lax.broadcasted_iota(jnp.int32, (128, 128), 0) // 16 == lax.broadcasted_iota(jnp.int32, (128, 128), 1) // 16
    fit = diag[0]
    for k in range(1, 8):
        fit = fit + diag[k]
    fit = jnp.where(same, fit, 0.0)
    total = fit[0:16, :]
    for j in range(1, 8):
        total = total + fit[j * 16 : (j + 1) * 16, :]
    for s in (64, 32, 16):
        total = total + pltpu.roll(total, s, 1)
    double = 2.0 * total.astype(BF16).astype(F32)
    return jnp.where(same, jnp.concatenate([double] * 8, 0), 0.0).astype(BF16)


def contract_second(b2, d, acc, clear):
    for rb in range(4):
        rows = slice(rb * 256, (rb + 1) * 256)
        term = jnp.dot(d[rows, :], rows_of(b2, 0, ROWS), preferred_element_type=F32)
        acc[rows, :] = term if clear else acc[rows, :] + term


def less_coulomb(b2, acc, fit, g):
    return acc[g * 128 : (g + 1) * 128, :] - jnp.dot(fit, rows_of(b2, g * 128, 128), preferred_element_type=F32)


def early_kernel(where, x_a, x_b, x_c, x_e, x_d, own, other, out, x_out, x2, b2, d, acc, diag, xs, os):
    for s, low, high in ((0, x_a, x_a), (1, x_b, x_b), (2, x_c, x_e), (3, x_d, x_d)):
        q = (where[1] - s) & 3
        for k in range(NCHIP):
            x2[k, q] = low[k]
            x2[NCHIP + k, q] = high[high.shape[0] - NCHIP + k]
    keep_x = pltpu.make_async_copy(x2, x_out, xs.at[0])
    keep_x.start()
    take_rows(b2, own, other, 0)
    fit = contract_first(x2, b2, d, diag)
    contract_second(b2, d, acc, True)
    puts = []
    for half in range(2):
        for g in range(half * 4, half * 4 + 4):
            acc[g * 128 : (g + 1) * 128, :] = less_coulomb(b2, acc, fit, g)
        rows = pl.ds(half * 512, 512)
        puts.append(pltpu.make_async_copy(acc.at[rows], out.at[rows], os.at[half]))
        puts[-1].start()
    keep_x.wait()
    for cp in puts:
        cp.wait()


def late_kernel(where, x_in, own, other, acc_in, out, x2, b_a, b_b, d, acc, diag, xs, os):
    c = where[0]
    get_x = pltpu.make_async_copy(x_in, x2, xs.at[0])
    get_x.start()
    take_rows(b_a, own, other, 0)
    take_rows(b_b, own, other, 1)
    get_x.wait()
    get_acc = pltpu.make_async_copy(acc_in, acc, os.at[0])
    get_acc.start()
    fit_a = contract_first(x2, b_a, d, diag)
    get_acc.wait()
    contract_second(b_a, d, acc, False)
    for g in range(8):
        acc[g * 128 : (g + 1) * 128, :] = less_coulomb(b_a, acc, fit_a, g)
    fit_b = contract_first(x2, b_b, d, diag)
    contract_second(b_b, d, acc, False)
    for g in range(8):
        value = less_coulomb(b_b, acc, fit_b, g).astype(BF16).reshape(2, OCC_DEV, HALF, NVIR)
        for k in range(2):
            rel, chip = g // 4, (g % 4) * 2 + k
            out[chip * 2 + (c ^ rel)] = value[k]


def final_kernel(where, occ, vir, trials, p_a, p_b, p_c, p_d, out):
    for s, ref in enumerate((p_a, p_b, p_c, p_d)):
        q = (where[0] - s) & 3
        lanes = pl.ds(pl.multiple_of(q * NVIR, NVIR), NVIR)
        delta = vir[...] - occ[where[1] * OCC_DEV + q]
        out[:, lanes] = delta * trials[:, lanes].astype(F32) - ref[...]


VMEM = pl.BlockSpec(memory_space=pltpu.VMEM)
LATE_MIB = 46
EARLY_MIB = 46
SMEM = pl.BlockSpec(memory_space=pltpu.SMEM)
ANY = pl.BlockSpec(memory_space=pl.ANY)
BLOCK = (16, OCC_DEV, HALF, NVIR)


def cost(count):
    return pl.CostEstimate(flops=count * 4 * ROWS * ROWS * NVIR, bytes_accessed=4 * ROWS * NVIR * 2, transcendentals=0)


def early(where, x, own, other):
    return pl.pallas_call(
        early_kernel,
        out_shape=[jax.ShapeDtypeStruct((ROWS, NVIR), F32), jax.ShapeDtypeStruct(BLOCK, BF16)],
        in_specs=[SMEM] + [VMEM] * 7,
        out_specs=[ANY, ANY],
        scratch_shapes=[
            pltpu.VMEM(BLOCK, BF16),
            pltpu.VMEM(BLOCK, BF16),
            pltpu.VMEM((ROWS, ROWS), BF16),
            pltpu.VMEM((ROWS, NVIR), F32),
            pltpu.VMEM((8, 128, 128), F32),
            pltpu.SemaphoreType.DMA((1,)),
            pltpu.SemaphoreType.DMA((2,)),
        ],
        cost_estimate=cost(1),
        compiler_params=pltpu.CompilerParams(vmem_limit_bytes=EARLY_MIB << 20),
        name="terms_early",
    )(where, *x, own[0], other[0])


def late(where, x2, own, other, acc):
    return pl.pallas_call(
        late_kernel,
        out_shape=jax.ShapeDtypeStruct(BLOCK, BF16),
        in_specs=[SMEM, ANY, VMEM, VMEM, ANY],
        out_specs=VMEM,
        scratch_shapes=[
            pltpu.VMEM(BLOCK, BF16),
            pltpu.VMEM(BLOCK, BF16),
            pltpu.VMEM(BLOCK, BF16),
            pltpu.VMEM((ROWS, ROWS), BF16),
            pltpu.VMEM((ROWS, NVIR), F32),
            pltpu.VMEM((8, 128, 128), F32),
            pltpu.SemaphoreType.DMA((1,)),
            pltpu.SemaphoreType.DMA((1,)),
        ],
        cost_estimate=cost(2),
        compiler_params=pltpu.CompilerParams(vmem_limit_bytes=LATE_MIB << 20),
        name="terms_late",
    )(where, x2, own[1], other[1], acc).reshape(16 * OCC_DEV, HALF, NVIR)


def final(where, occ, vir, trials, pieces):
    return pl.pallas_call(
        final_kernel,
        out_shape=jax.ShapeDtypeStruct((NVEC, PAIRS), F32),
        in_specs=[SMEM, SMEM] + [VMEM] * 6,
        out_specs=VMEM,
        compiler_params=pltpu.CompilerParams(vmem_limit_bytes=16 << 20),
        name="final",
    )(where, occ, vir.reshape(1, NVIR), trials, *pieces)


def ring(n, s):
    return [(i, (i + s) % n) for i in range(n)]


def body(fit_rows, trials, occ_energy, vir_energy):
    core = lax.axis_index("c").astype(jnp.int32)
    z = (lax.axis_index("z") + 2 * lax.axis_index("yh")).astype(jnp.int32) & 3
    where = jnp.stack([core, z])
    mine = [lax.dynamic_slice(trials, (half * HALF, z * NVIR), (HALF, NVIR)) for half in (core, 1 - core)]
    mine = jnp.broadcast_to(jnp.concatenate(mine, 1)[None], (NCHIP, HALF, 2 * NVIR))
    own, other, rows = [], [], fit_rows
    first = 0
    for t, steps in enumerate(STEPS):
        count = steps * HALF
        send = rows[first : first + NCHIP * count].reshape(NCHIP, count, PAIRS)
        if t == 0:
            send = jnp.concatenate([send, mine], 2)
        own.append(lax.all_to_all(send, CHIPS, 0, 0, tiled=True))
        first += NCHIP * count
        rows = lax.optimization_barrier(rows)
        other.append(lax.ppermute(own[t], "c", ring(2, 1)))
    x_own, x_send = own[0][:, :, PAIRS : PAIRS + NVIR], own[0][:, :, PAIRS + NVIR :]
    x_other = lax.ppermute(x_send, "c", ring(2, 1))
    x = jnp.concatenate([x_own, x_other])
    x_far = [lax.ppermute(x_own, "yh", ring(2, 1))]
    x_far.append(lax.ppermute(x_other, "z", ring(4, 2)))
    x = [x, lax.ppermute(x, "z", ring(4, 1)), *x_far, lax.ppermute(x, "z", ring(4, 3))]
    acc, x2 = early(where, x, own, other)
    acc = late(where, x2, own, other, acc)
    parts = lax.all_to_all(acc, MOST, 0, 0, tiled=True)
    part = jnp.sum(parts.reshape(NCHIP, 2, 4, HALF, NVIR).astype(F32), (0, 2)).reshape(NVEC, NVIR)
    part = part + lax.ppermute(part, "yh", ring(2, 1))
    pieces = [part] + [lax.ppermute(part, "z", ring(4, s)) for s in (1, 2, 3)]
    place = jnp.stack([lax.axis_index("z"), lax.axis_index(WIDE)]).astype(jnp.int32)
    return final(place, occ_energy, vir_energy, trials, pieces)


def solution(mesh):
    fine = Mesh(mesh.devices.reshape(4, 2, 2, 2, 4), ("x", "yl", "c", "yh", "z"))
    in_specs = (P(NARROW, WIDE), P(None, WIDE), P(), P())
    return jax.shard_map(body, mesh=fine, in_specs=in_specs, out_specs=P(None, WIDE), check_vma=False)
```

```python
import jax
import jax.numpy as jnp
from jax import lax
from jax.experimental import pallas as pl
from jax.experimental.pallas import tpu as pltpu
from jax.sharding import Mesh, PartitionSpec as P

NOCC = 64
NVIR = 768
NVEC = 32
NCHIP = 8
OCC_DEV = 4
PAIRS = OCC_DEV * NVIR
HALF = 16
STEPS = (2, 1)
ROWS = NOCC * HALF

F32 = jnp.float32
BF16 = jnp.bfloat16

CHIPS = ("x", "yl")
WIDE = ("x", "yl", "c")
NARROW = ("yh", "z")
MOST = ("x", "yl", "c", "z")


def swap_blocks(tile):
    v = [tile[j * 16 : (j + 1) * 16] for j in range(8)]
    lane = lax.broadcasted_iota(jnp.int32, (16, 128), 1)
    for s in (4, 2, 1):
        bit = (lane & (16 * s)) != 0
        new = list(v)
        for j in range(8):
            if j & s:
                continue
            lo, hi = v[j], v[j + s]
            new[j] = jnp.where(bit, pltpu.roll(hi, 16 * s, 1), lo)
            new[j + s] = jnp.where(bit, hi, pltpu.roll(lo, 128 - 16 * s, 1))
        v = new
    return jnp.concatenate(v, 0)


def rows_of(ref, start, count):
    return ref[start // 64 : (start + count) // 64].reshape(count, NVIR)


def get_rows(b2, own, other, step, sems):
    copies = []
    for rel, src in enumerate((own, other)):
        for q in range(OCC_DEV):
            there = b2.at[pl.ds(rel * NCHIP, NCHIP), q]
            here = src.at[:, pl.ds(step * HALF, HALF), pl.ds(q * NVIR, NVIR)]
            copies.append(pltpu.make_async_copy(here, there, sems.at[step, rel, q]))
    return copies


def take_rows(b2, own, other):
    for rel, src in enumerate((own, other)):
        for chip in range(NCHIP):
            for q in range(OCC_DEV):
                b2[rel * NCHIP + chip, q] = src[chip, :, q * NVIR : (q + 1) * NVIR]


def contract_first(x2, b2, d, diag):
    for g, rb in ((g, rb) for g in range(4) for rb in range(4)):
        lhs, rhs = rows_of(x2, rb * 256, 256), rows_of(b2, g * 256, 256)
        inter = lax.dot_general(lhs, rhs, (((1,), (1,)), ((), ())), preferred_element_type=F32)
        for a in range(2):
            for h in range(2):
                ig, jg = g * 2 + h, rb * 2 + a
                tile = inter[a * 128 : (a + 1) * 128, h * 128 : (h + 1) * 128]
                if ig == jg:
                    diag[ig] = tile
                d[ig * 128 : (ig + 1) * 128, jg * 128 : (jg + 1) * 128] = swap_blocks(tile).astype(BF16)
    same = lax.broadcasted_iota(jnp.int32, (128, 128), 0) // 16 == lax.broadcasted_iota(jnp.int32, (128, 128), 1) // 16
    fit = diag[0]
    for k in range(1, 8):
        fit = fit + diag[k]
    fit = jnp.where(same, fit, 0.0)
    total = fit[0:16, :]
    for j in range(1, 8):
        total = total + fit[j * 16 : (j + 1) * 16, :]
    for s in (64, 32, 16):
        total = total + pltpu.roll(total, s, 1)
    double = 2.0 * total.astype(BF16).astype(F32)
    return jnp.where(same, jnp.concatenate([double] * 8, 0), 0.0).astype(BF16)


def contract_second(b2, d, acc, clear):
    for rb in range(4):
        rows = slice(rb * 256, (rb + 1) * 256)
        term = jnp.dot(d[rows, :], rows_of(b2, 0, ROWS), preferred_element_type=F32)
        acc[rows, :] = term if clear else acc[rows, :] + term


def less_coulomb(b2, acc, fit, g):
    return acc[g * 128 : (g + 1) * 128, :] - jnp.dot(fit, rows_of(b2, g * 128, 128), preferred_element_type=F32)


def early_kernel(where, x_a, x_b, x_c, x_d, own, other, out, x_out, x2, b_a, b_b, d, acc, diag, xs, bs, os):
    rows0 = get_rows(b_a, own, other, 0, bs)
    rows1 = get_rows(b_b, own, other, 1, bs)
    for cp in rows0:
        cp.start()
    for s, ref in enumerate((x_a, x_b, x_c, x_d)):
        q = (where[1] - s) & 3
        for k in range(16):
            x2[k, q] = ref[k]
    for cp in rows0:
        cp.wait()
    for cp in rows1:
        cp.start()
    keep_x = pltpu.make_async_copy(x2, x_out, xs.at[0])
    keep_x.start()
    fit = contract_first(x2, b_a, d, diag)
    contract_second(b_a, d, acc, True)
    for g in range(8):
        acc[g * 128 : (g + 1) * 128, :] = less_coulomb(b_a, acc, fit, g)
    for cp in rows1:
        cp.wait()
    fit = contract_first(x2, b_b, d, diag)
    contract_second(b_b, d, acc, False)
    puts = []
    for half in range(2):
        for g in range(half * 4, half * 4 + 4):
            acc[g * 128 : (g + 1) * 128, :] = less_coulomb(b_b, acc, fit, g)
        rows = pl.ds(half * 512, 512)
        puts.append(pltpu.make_async_copy(acc.at[rows], out.at[rows], os.at[half]))
        puts[-1].start()
    keep_x.wait()
    for cp in puts:
        cp.wait()


def late_kernel(where, x_in, own, other, acc_in, out, x2, b2, d, acc, diag, xs, os):
    c = where[0]
    get_x = pltpu.make_async_copy(x_in, x2, xs.at[0])
    get_x.start()
    take_rows(b2, own, other)
    get_x.wait()
    get_acc = pltpu.make_async_copy(acc_in, acc, os.at[0])
    get_acc.start()
    fit = contract_first(x2, b2, d, diag)
    get_acc.wait()
    contract_second(b2, d, acc, False)
    for g in range(8):
        value = less_coulomb(b2, acc, fit, g).astype(BF16).reshape(2, OCC_DEV, HALF, NVIR)
        for k in range(2):
            rel, chip = g // 4, (g % 4) * 2 + k
            out[chip * 2 + (c ^ rel)] = value[k]


def final_kernel(where, occ, vir, trials, p_a, p_b, p_c, p_d, out):
    for s, ref in enumerate((p_a, p_b, p_c, p_d)):
        q = (where[0] - s) & 3
        lanes = pl.ds(pl.multiple_of(q * NVIR, NVIR), NVIR)
        delta = vir[...] - occ[where[1] * OCC_DEV + q]
        out[:, lanes] = delta * trials[:, lanes].astype(F32) - ref[...]


VMEM = pl.BlockSpec(memory_space=pltpu.VMEM)
LATE_MIB = 50
EARLY_MIB = 50
SMEM = pl.BlockSpec(memory_space=pltpu.SMEM)
ANY = pl.BlockSpec(memory_space=pl.ANY)
BLOCK = (16, OCC_DEV, HALF, NVIR)


def cost(count):
    return pl.CostEstimate(flops=count * 4 * ROWS * ROWS * NVIR, bytes_accessed=4 * ROWS * NVIR * 2, transcendentals=0)


def early(where, x, own, other):
    return pl.pallas_call(
        early_kernel,
        out_shape=[jax.ShapeDtypeStruct((ROWS, NVIR), F32), jax.ShapeDtypeStruct(BLOCK, BF16)],
        in_specs=[SMEM] + [VMEM] * 4 + [ANY] * 2,
        out_specs=[ANY, ANY],
        scratch_shapes=[
            pltpu.VMEM(BLOCK, BF16),
            pltpu.VMEM(BLOCK, BF16),
            pltpu.VMEM(BLOCK, BF16),
            pltpu.VMEM((ROWS, ROWS), BF16),
            pltpu.VMEM((ROWS, NVIR), F32),
            pltpu.VMEM((8, 128, 128), F32),
            pltpu.SemaphoreType.DMA((1,)),
            pltpu.SemaphoreType.DMA((2, 2, 4)),
            pltpu.SemaphoreType.DMA((2,)),
        ],
        cost_estimate=cost(2),
        compiler_params=pltpu.CompilerParams(vmem_limit_bytes=EARLY_MIB << 20),
        name="terms_early",
    )(where, *x, own[0], other[0])


def late(where, x2, own, other, acc):
    return pl.pallas_call(
        late_kernel,
        out_shape=jax.ShapeDtypeStruct(BLOCK, BF16),
        in_specs=[SMEM, ANY, VMEM, VMEM, ANY],
        out_specs=VMEM,
        scratch_shapes=[
            pltpu.VMEM(BLOCK, BF16),
            pltpu.VMEM(BLOCK, BF16),
            pltpu.VMEM((ROWS, ROWS), BF16),
            pltpu.VMEM((ROWS, NVIR), F32),
            pltpu.VMEM((8, 128, 128), F32),
            pltpu.SemaphoreType.DMA((1,)),
            pltpu.SemaphoreType.DMA((1,)),
        ],
        cost_estimate=cost(1),
        compiler_params=pltpu.CompilerParams(vmem_limit_bytes=LATE_MIB << 20),
        name="terms_late",
    )(where, x2, own[1], other[1], acc).reshape(16 * OCC_DEV, HALF, NVIR)


def final(where, occ, vir, trials, pieces):
    return pl.pallas_call(
        final_kernel,
        out_shape=jax.ShapeDtypeStruct((NVEC, PAIRS), F32),
        in_specs=[SMEM, SMEM] + [VMEM] * 6,
        out_specs=VMEM,
        compiler_params=pltpu.CompilerParams(vmem_limit_bytes=16 << 20),
        name="final",
    )(where, occ, vir.reshape(1, NVIR), trials, *pieces)


def ring(n, s):
    return [(i, (i + s) % n) for i in range(n)]


def body(fit_rows, trials, occ_energy, vir_energy):
    core = lax.axis_index("c").astype(jnp.int32)
    z = lax.axis_index("z").astype(jnp.int32)
    where = jnp.stack([core, z])
    mine = [lax.dynamic_slice(trials, (half * HALF, z * NVIR), (HALF, NVIR)) for half in (core, 1 - core)]
    mine = jnp.broadcast_to(jnp.concatenate(mine, 1)[None], (NCHIP, HALF, 2 * NVIR))
    both = lax.all_to_all(mine, CHIPS, 0, 0, tiled=True)
    own, other, rows = [], [], fit_rows
    first = 0
    for t, steps in enumerate(STEPS):
        count = steps * HALF
        send = rows[first : first + NCHIP * count].reshape(NCHIP, count, PAIRS)
        own.append(lax.all_to_all(send, CHIPS, 0, 0, tiled=True))
        first += NCHIP * count
        rows = lax.optimization_barrier(rows)
        other.append(lax.ppermute(own[t], "c", ring(2, 1)))
    x_own, x_send = both[:, :, :NVIR], both[:, :, NVIR:]
    x_other = lax.ppermute(x_send, "c", ring(2, 1))
    x = [jnp.concatenate([x_own, x_other])]
    x = x + [lax.ppermute(x[0], "z", ring(4, s)) for s in (1, 2, 3)]
    acc, x2 = early(where, x, own, other)
    acc = late(where, x2, own, other, acc)
    parts = lax.all_to_all(acc, MOST, 0, 0, tiled=True)
    part = jnp.sum(parts.reshape(NCHIP, 2, 4, HALF, NVIR).astype(F32), (0, 2)).reshape(NVEC, NVIR)
    part = part + lax.ppermute(part, "yh", ring(2, 1))
    pieces = [part] + [lax.ppermute(part, "z", ring(4, s)) for s in (1, 2, 3)]
    place = jnp.stack([lax.axis_index("z"), lax.axis_index(WIDE)]).astype(jnp.int32)
    return final(place, occ_energy, vir_energy, trials, pieces)


def solution(mesh):
    fine = Mesh(mesh.devices.reshape(4, 2, 2, 2, 4), ("x", "yl", "c", "yh", "z"))
    in_specs = (P(NARROW, WIDE), P(None, WIDE), P(), P())
    return jax.shard_map(body, mesh=fine, in_specs=in_specs, out_specs=P(None, WIDE), check_vma=False)
```

```python
import jax
import jax.numpy as jnp
from jax import lax
from jax.experimental import pallas as pl
from jax.experimental.pallas import tpu as pltpu
from jax.sharding import Mesh, PartitionSpec as P

NOCC = 64
NVIR = 768
NVEC = 32
NCHIP = 8
OCC_DEV = 4
PAIRS = OCC_DEV * NVIR
HALF = 16
STEPS = (2, 1)
ROWS = NOCC * HALF

F32 = jnp.float32
BF16 = jnp.bfloat16

CHIPS = ("x", "yl")
WIDE = ("x", "yl", "c")
NARROW = ("yh", "z")
MOST = ("x", "yl", "c", "z")


def swap_blocks(tile):
    v = [tile[j * 16 : (j + 1) * 16] for j in range(8)]
    lane = lax.broadcasted_iota(jnp.int32, (16, 128), 1)
    for s in (4, 2, 1):
        bit = (lane & (16 * s)) != 0
        new = list(v)
        for j in range(8):
            if j & s:
                continue
            lo, hi = v[j], v[j + s]
            new[j] = jnp.where(bit, pltpu.roll(hi, 16 * s, 1), lo)
            new[j + s] = jnp.where(bit, hi, pltpu.roll(lo, 128 - 16 * s, 1))
        v = new
    return jnp.concatenate(v, 0)


def rows_of(ref, start, count):
    return ref[start // 64 : (start + count) // 64].reshape(count, NVIR)


def get_rows(b2, own, other, step, sems):
    copies = []
    for rel, src in enumerate((own, other)):
        for q in range(OCC_DEV):
            there = b2.at[pl.ds(rel * NCHIP, NCHIP), q]
            here = src.at[:, pl.ds(step * HALF, HALF), pl.ds(q * NVIR, NVIR)]
            copies.append(pltpu.make_async_copy(here, there, sems.at[step, rel, q]))
    return copies


def take_rows(b2, own, other):
    for rel, src in enumerate((own, other)):
        for chip in range(NCHIP):
            for q in range(OCC_DEV):
                b2[rel * NCHIP + chip, q] = src[chip, :, q * NVIR : (q + 1) * NVIR]


def contract_first(x2, b2, d, diag):
    for g, rb in ((g, rb) for g in range(4) for rb in range(4)):
        lhs, rhs = rows_of(x2, rb * 256, 256), rows_of(b2, g * 256, 256)
        inter = lax.dot_general(lhs, rhs, (((1,), (1,)), ((), ())), preferred_element_type=F32)
        for a in range(2):
            for h in range(2):
                ig, jg = g * 2 + h, rb * 2 + a
                tile = inter[a * 128 : (a + 1) * 128, h * 128 : (h + 1) * 128]
                if ig == jg:
                    diag[ig] = tile
                d[ig * 128 : (ig + 1) * 128, jg * 128 : (jg + 1) * 128] = swap_blocks(tile).astype(BF16)
    same = lax.broadcasted_iota(jnp.int32, (128, 128), 0) // 16 == lax.broadcasted_iota(jnp.int32, (128, 128), 1) // 16
    fit = diag[0]
    for k in range(1, 8):
        fit = fit + diag[k]
    fit = jnp.where(same, fit, 0.0)
    total = fit[0:16, :]
    for j in range(1, 8):
        total = total + fit[j * 16 : (j + 1) * 16, :]
    for s in (64, 32, 16):
        total = total + pltpu.roll(total, s, 1)
    double = 2.0 * total.astype(BF16).astype(F32)
    return jnp.where(same, jnp.concatenate([double] * 8, 0), 0.0).astype(BF16)


def contract_second(b2, d, acc, clear):
    for rb in range(4):
        rows = slice(rb * 256, (rb + 1) * 256)
        term = jnp.dot(d[rows, :], rows_of(b2, 0, ROWS), preferred_element_type=F32)
        acc[rows, :] = term if clear else acc[rows, :] + term


def less_coulomb(b2, acc, fit, g):
    return acc[g * 128 : (g + 1) * 128, :] - jnp.dot(fit, rows_of(b2, g * 128, 128), preferred_element_type=F32)


def early_kernel(where, x_a, x_b, x_c, x_d, own, other, out, x_out, x2, b_a, b_b, d, acc, diag, xs, bs, os):
    rows0 = get_rows(b_a, own, other, 0, bs)
    rows1 = get_rows(b_b, own, other, 1, bs)
    for cp in rows0:
        cp.start()
    for s, ref in enumerate((x_a, x_b, x_c, x_d)):
        q = (where[1] - s) & 3
        for k in range(16):
            rel, cross, back = k // 8, (k // 4) % 2, k % 4
            chip = ((where[2] - back) & 3) * 2 + (where[3] ^ cross)
            x2[rel * NCHIP + chip, q] = ref[k]
    for cp in rows0:
        cp.wait()
    for cp in rows1:
        cp.start()
    keep_x = pltpu.make_async_copy(x2, x_out, xs.at[0])
    keep_x.start()
    fit = contract_first(x2, b_a, d, diag)
    contract_second(b_a, d, acc, True)
    for g in range(8):
        acc[g * 128 : (g + 1) * 128, :] = less_coulomb(b_a, acc, fit, g)
    for cp in rows1:
        cp.wait()
    fit = contract_first(x2, b_b, d, diag)
    contract_second(b_b, d, acc, False)
    puts = []
    for half in range(2):
        for g in range(half * 4, half * 4 + 4):
            acc[g * 128 : (g + 1) * 128, :] = less_coulomb(b_b, acc, fit, g)
        rows = pl.ds(half * 512, 512)
        puts.append(pltpu.make_async_copy(acc.at[rows], out.at[rows], os.at[half]))
        puts[-1].start()
    keep_x.wait()
    for cp in puts:
        cp.wait()


def late_kernel(where, x_in, own, other, acc_in, out, x2, b2, d, acc, diag, xs, os):
    c = where[0]
    get_x = pltpu.make_async_copy(x_in, x2, xs.at[0])
    get_x.start()
    take_rows(b2, own, other)
    get_x.wait()
    get_acc = pltpu.make_async_copy(acc_in, acc, os.at[0])
    get_acc.start()
    fit = contract_first(x2, b2, d, diag)
    get_acc.wait()
    contract_second(b2, d, acc, False)
    for g in range(8):
        value = less_coulomb(b2, acc, fit, g).astype(BF16).reshape(2, OCC_DEV, HALF, NVIR)
        for k in range(2):
            rel, chip = g // 4, (g % 4) * 2 + k
            out[chip * 2 + (c ^ rel)] = value[k]


def final_kernel(where, occ, vir, trials, p_a, p_b, p_c, p_d, out):
    for s, ref in enumerate((p_a, p_b, p_c, p_d)):
        q = (where[0] - s) & 3
        lanes = pl.ds(pl.multiple_of(q * NVIR, NVIR), NVIR)
        delta = vir[...] - occ[where[1] * OCC_DEV + q]
        out[:, lanes] = delta * trials[:, lanes].astype(F32) - ref[...]


VMEM = pl.BlockSpec(memory_space=pltpu.VMEM)
LATE_MIB = 50
EARLY_MIB = 52
SMEM = pl.BlockSpec(memory_space=pltpu.SMEM)
ANY = pl.BlockSpec(memory_space=pl.ANY)
BLOCK = (16, OCC_DEV, HALF, NVIR)


def cost(count):
    return pl.CostEstimate(flops=count * 4 * ROWS * ROWS * NVIR, bytes_accessed=4 * ROWS * NVIR * 2, transcendentals=0)


def early(where, x, own, other):
    return pl.pallas_call(
        early_kernel,
        out_shape=[jax.ShapeDtypeStruct((ROWS, NVIR), F32), jax.ShapeDtypeStruct(BLOCK, BF16)],
        in_specs=[SMEM] + [VMEM] * 4 + [ANY] * 2,
        out_specs=[ANY, ANY],
        scratch_shapes=[
            pltpu.VMEM(BLOCK, BF16),
            pltpu.VMEM(BLOCK, BF16),
            pltpu.VMEM(BLOCK, BF16),
            pltpu.VMEM((ROWS, ROWS), BF16),
            pltpu.VMEM((ROWS, NVIR), F32),
            pltpu.VMEM((8, 128, 128), F32),
            pltpu.SemaphoreType.DMA((1,)),
            pltpu.SemaphoreType.DMA((2, 2, 4)),
            pltpu.SemaphoreType.DMA((2,)),
        ],
        cost_estimate=cost(2),
        compiler_params=pltpu.CompilerParams(vmem_limit_bytes=EARLY_MIB << 20),
        name="terms_early",
    )(where, *x, own[0], other[0])


def late(where, x2, own, other, acc):
    return pl.pallas_call(
        late_kernel,
        out_shape=jax.ShapeDtypeStruct(BLOCK, BF16),
        in_specs=[SMEM, ANY, VMEM, VMEM, ANY],
        out_specs=VMEM,
        scratch_shapes=[
            pltpu.VMEM(BLOCK, BF16),
            pltpu.VMEM(BLOCK, BF16),
            pltpu.VMEM((ROWS, ROWS), BF16),
            pltpu.VMEM((ROWS, NVIR), F32),
            pltpu.VMEM((8, 128, 128), F32),
            pltpu.SemaphoreType.DMA((1,)),
            pltpu.SemaphoreType.DMA((1,)),
        ],
        cost_estimate=cost(1),
        compiler_params=pltpu.CompilerParams(vmem_limit_bytes=LATE_MIB << 20),
        name="terms_late",
    )(where, x2, own[1], other[1], acc).reshape(16 * OCC_DEV, HALF, NVIR)


def final(where, occ, vir, trials, pieces):
    return pl.pallas_call(
        final_kernel,
        out_shape=jax.ShapeDtypeStruct((NVEC, PAIRS), F32),
        in_specs=[SMEM, SMEM] + [VMEM] * 6,
        out_specs=VMEM,
        compiler_params=pltpu.CompilerParams(vmem_limit_bytes=16 << 20),
        name="final",
    )(where, occ, vir.reshape(1, NVIR), trials, *pieces)


def ring(n, s):
    return [(i, (i + s) % n) for i in range(n)]


def body(fit_rows, trials, occ_energy, vir_energy):
    core = lax.axis_index("c").astype(jnp.int32)
    z = lax.axis_index("z").astype(jnp.int32)
    where = jnp.stack([core, z, lax.axis_index("x").astype(jnp.int32), lax.axis_index("yl").astype(jnp.int32)])
    mine = [lax.dynamic_slice(trials, (half * HALF, z * NVIR), (HALF, NVIR)) for half in (core, 1 - core)]
    x = jnp.concatenate(mine, 1)[None]
    x = jnp.concatenate([x] + [lax.ppermute(x, "x", ring(4, s)) for s in (1, 2, 3)])
    x = jnp.concatenate([x, lax.ppermute(x, "yl", ring(2, 1))])
    x = jnp.concatenate([x[:, :, :NVIR], lax.ppermute(x[:, :, NVIR:], "c", ring(2, 1))])
    x = [x] + [lax.ppermute(x, "z", ring(4, s)) for s in (1, 2, 3)]
    own, other, rows = [], [], fit_rows
    first = 0
    for t, steps in enumerate(STEPS):
        count = steps * HALF
        send = rows[first : first + NCHIP * count].reshape(NCHIP, count, PAIRS)
        own.append(lax.all_to_all(send, CHIPS, 0, 0, tiled=True))
        first += NCHIP * count
        rows = lax.optimization_barrier(rows)
        other.append(lax.ppermute(own[t], "c", ring(2, 1)))
    acc, x2 = early(where, x, own, other)
    acc = late(where, x2, own, other, acc)
    parts = lax.all_to_all(acc, MOST, 0, 0, tiled=True)
    part = jnp.sum(parts.reshape(NCHIP, 2, 4, HALF, NVIR).astype(F32), (0, 2)).reshape(NVEC, NVIR)
    part = part + lax.ppermute(part, "yh", ring(2, 1))
    pieces = [part] + [lax.ppermute(part, "z", ring(4, s)) for s in (1, 2, 3)]
    place = jnp.stack([lax.axis_index("z"), lax.axis_index(WIDE)]).astype(jnp.int32)
    return final(place, occ_energy, vir_energy, trials, pieces)


def solution(mesh):
    fine = Mesh(mesh.devices.reshape(4, 2, 2, 2, 4), ("x", "yl", "c", "yh", "z"))
    in_specs = (P(NARROW, WIDE), P(None, WIDE), P(), P())
    return jax.shard_map(body, mesh=fine, in_specs=in_specs, out_specs=P(None, WIDE), check_vma=False)
```
